32 devices in a mesh: real: 2 (over x), bx: 4 (over y, core), by: 4 (over z).
Axes of the slice: x: 2, y: 2, z: 4, core: 2. Of those that a mesh axis runs over, the one named last changes fastest.
Arguments:
- current: float32 [2, 12, 3, 8, 32, 128], P('real', None, None, 'bx', 'by'), may hold values from -110 to 110
- previous: float32 [2, 12, 3, 8, 32, 128], P('real', None, None, 'bx', 'by'), may hold values from -110 to 110
- element_stiffness: float32 [24, 24], replicated, may hold values from -0.75 to 1.25, as said below
- preconditioner: float32 [2, 3, 8, 32, 128], P('real', None, 'bx', 'by'), may hold values from 0.04 to 0.16
- modulus: float32 [8, 32, 128], P('bx', 'by'), may hold values from 0.3 to 9.1
- density: float32 [8, 32, 128], P('bx', 'by'), may hold values from 0.5 to 2
- solid: int32 [2, 8, 32, 128], P('real', 'bx', 'by'), may hold values from 0 to 1, as said below
- clamped: int32 [8, 32], P('bx', 'by'), may hold values 0 or 1
Outputs:
- gram_stiff: float32 [2, 36, 36], P('real')
- gram_mass: float32 [2, 36, 36], P('real')
- search_block: float32 [2, 12, 3, 8, 32, 128], P('real', None, None, 'bx', 'by')
- sensitivity: float32 [8, 32, 128], P('bx', 'by', 'real')
The draws below stay inside these ranges and needn't reach their ends.
Inputs may be any that keep to these rules, and one draw needn't show every extreme that they name: `element_stiffness`: symmetric positive definite: the stiffness of a trilinear brick of unit edge for unit modulus and a Poisson ratio between 0.25 and 0.35, divided by its diagonal entry, plus a small positive definite part. 1 marks a solid element of that realization; a realization's solid elements include those of every realization before it. `clamped`: 1 marks a bottom-face node held in all three directions.
All inputs are finite; a program needn't handle non-finite values. No bound on the sum of `clamped` on one device may be relied on, other than what follows from the above.
Results may differ from the reference program's by a relative error of at most 0.00013.
Values sent between devices are 32-bit elements; how exact they have to be, the bound alone decides.
No kernel may reach another device: no remote copies, remote signals or barrier semaphores. Data moves between devices by JAX's collectives and lax.ppermute only.
A program may use at most 64 MiB of HBM per device.

```python
import math
import jax
import jax.numpy as jnp
import numpy as np
from jax import lax

NZ = 128
COLS = 12
REALS = 2
GX = 8
GY = 32


def mixed_block(key, salt_code):
    key_base = jax.random.fold_in(key, salt_code)
    key_noise, key_mix = jax.random.split(key_base, 2)
    block_shape = (REALS, COLS, 3, GX, GY, NZ)
    noise_field = jnp.clip(jax.random.normal(key_noise, block_shape, jnp.float32), -4.0, 4.0)
    mixing = jnp.eye(COLS, dtype=jnp.float32) + jnp.clip(0.12 * jax.random.normal(key_mix, (COLS, COLS), jnp.float32), -0.5, 0.5)
    return jnp.einsum('rkdxyz,kj->rjdxyz', noise_field, mixing)


def draw_current(key, part):
    return mixed_block(key, 101)


def draw_previous(key, part):
    current_part = mixed_block(key, 101)
    fresh_part = mixed_block(key, 202)
    key_turn = jax.random.fold_in(key, 303)
    turning = jnp.eye(COLS, dtype=jnp.float32) + jnp.clip(0.1 * jax.random.normal(key_turn, (COLS, COLS), jnp.float32), -0.3, 0.3)
    blended = 0.6 * jnp.einsum('rkdxyz,kj->rjdxyz', current_part, turning) + 0.8 * fresh_part
    return jnp.clip(blended, -110.0, 110.0)


def brick_tables():
    offset = 0.5 / math.sqrt(3.0)
    places = [0.5 - offset, 0.5 + offset]
    tables = np.zeros((8, 6, 24), np.float32)
    point_index = 0
    for place_x in places:
        for place_y in places:
            for place_z in places:
                for corner_x in (0, 1):
                    for corner_y in (0, 1):
                        for corner_z in (0, 1):
                            column = 3 * (4 * corner_x + 2 * corner_y + corner_z)
                            value_x = place_x if corner_x else 1.0 - place_x
                            value_y = place_y if corner_y else 1.0 - place_y
                            value_z = place_z if corner_z else 1.0 - place_z
                            slope_x = 1.0 if corner_x else -1.0
                            slope_y = 1.0 if corner_y else -1.0
                            slope_z = 1.0 if corner_z else -1.0
                            grad_x = slope_x * value_y * value_z
                            grad_y = value_x * slope_y * value_z
                            grad_z = value_x * value_y * slope_z
                            tables[point_index, 0, column] = grad_x
                            tables[point_index, 1, column + 1] = grad_y
                            tables[point_index, 2, column + 2] = grad_z
                            tables[point_index, 3, column] = grad_y
                            tables[point_index, 3, column + 1] = grad_x
                            tables[point_index, 4, column + 1] = grad_z
                            tables[point_index, 4, column + 2] = grad_y
                            tables[point_index, 5, column + 2] = grad_x
                            tables[point_index, 5, column] = grad_z
                point_index += 1
    return tables


def draw_element_stiffness(key, part):
    key_ratio, key_extra = jax.random.split(jax.random.fold_in(key, 7))
    poisson_ratio = jax.random.uniform(key_ratio, (), jnp.float32, 0.25, 0.35)
    lame_first = poisson_ratio / ((1.0 + poisson_ratio) * (1.0 - 2.0 * poisson_ratio))
    shear_modulus = 0.5 / (1.0 + poisson_ratio)
    identity_three = jnp.eye(3, dtype=jnp.float32)
    zeros_three = jnp.zeros((3, 3), jnp.float32)
    upper_block = jnp.ones((3, 3), jnp.float32) * lame_first + 2.0 * shear_modulus * identity_three
    material = jnp.concatenate([jnp.concatenate([upper_block, zeros_three], 1), jnp.concatenate([zeros_three, shear_modulus * identity_three], 1)], 0)
    tables = jnp.asarray(brick_tables())
    brick_matrix = jnp.einsum('gsi,st,gtj->ij', tables, material, tables, precision=lax.Precision.HIGHEST) / 8.0
    brick_matrix = 0.5 * (brick_matrix + brick_matrix.T)
    brick_matrix = brick_matrix / brick_matrix[0, 0]
    extra_part = jnp.clip(jax.random.normal(key_extra, (24, 24), jnp.float32), -2.0, 2.0)
    positive_part = jnp.dot(extra_part, extra_part.T, precision=lax.Precision.HIGHEST)
    positive_part = 0.5 * (positive_part + positive_part.T)
    return brick_matrix + 0.05 * jnp.eye(24, dtype=jnp.float32) + 0.002 * positive_part


def draw_modulus(key, part):
    key_rough = jax.random.fold_in(key, 11)
    ramp_x = jnp.exp(jnp.log(3.0) * (jnp.arange(GX, dtype=jnp.float32) + 0.5) / GX)[:, None, None]
    reach_log = 0.7
    rough_part = jnp.exp(jax.random.uniform(key_rough, (GX, GY, NZ), jnp.float32, -reach_log, reach_log))
    return rough_part * ramp_x


def draw_solid(key, part):
    key_levels = jax.random.fold_in(key, 13)
    levels = jax.random.randint(key_levels, (GX, GY, NZ), 0, 100)
    cutoff = 45 + 40 * jnp.arange(REALS, dtype=jnp.int32) // max(REALS - 1, 1)
    return (levels[None] < cutoff[:, None, None, None]).astype(jnp.int32)


def plant(drawn, own_key, least, high):
    dims = drawn.shape
    spot = [jax.random.randint(jax.random.fold_in(own_key, axis), (), 0, dims[axis]) for axis in range(len(dims))]
    drawn = drawn.at[tuple(spot)].set(least)
    longest = dims.index(max(dims))
    spot[longest] = (spot[longest] + 1) % dims[longest]
    return drawn.at[tuple(spot)].set(high)


def shard_levels(rng, extent, cuts, low, largest):
    def one(axis_at, parts):
        steps = jax.random.uniform(jax.random.fold_in(jax.random.fold_in(rng, 6), axis_at), (parts,), jnp.float32, low / len(cuts), largest / len(cuts))
        return jnp.repeat(jnp.exp(steps), extent[axis_at] // parts).reshape((-1,) + (1,) * (len(extent) - axis_at - 1))

    gain = one(*cuts[0])
    for cut in cuts[1:]:
        gain = gain * one(*cut)
    return gain


def setup_inputs(seed: int = 0) -> dict:
    seeds = jax.random.split(jax.random.key(seed), 9)
    current = draw_current(jax.random.fold_in(seeds[8], 71), 0)
    previous = draw_previous(jax.random.fold_in(seeds[8], 71), 0)
    element_stiffness = draw_element_stiffness(jax.random.fold_in(seeds[8], 71), 0)
    preconditioner = jnp.clip(jnp.exp(math.log(0.16) - 1.3862944 * jax.random.uniform(seeds[3], (REALS, 3, GX, GY, NZ), jnp.float32) ** shard_levels(seeds[3], (REALS, 3, GX, GY, NZ), ((0, 2), (2, 4), (3, 4)), -0.2, 0.2)), 0.04, 0.16)
    modulus = draw_modulus(jax.random.fold_in(seeds[8], 71), 0)
    density = jnp.clip(jnp.exp(math.log(2.0) - 1.3862944 * jax.random.uniform(seeds[5], (GX, GY, NZ), jnp.float32) ** shard_levels(seeds[5], (GX, GY, NZ), ((0, 4), (1, 4)), -0.2, 0.2)), 0.5, 2.0)
    solid = draw_solid(jax.random.fold_in(seeds[8], 71), 0)
    clamped = plant((jax.random.randint(seeds[7], (GX, GY), 0, 4) < 1).astype(jnp.int32), jax.random.fold_in(seeds[7], 1), 0, 1)
    return dict(current=current, previous=previous, element_stiffness=element_stiffness, preconditioner=preconditioner, modulus=modulus, density=density, solid=solid, clamped=clamped)


highest = lax.Precision.HIGHEST
soft_power = 4.0
corner_list = [(0, 0, 0), (0, 0, 1), (0, 1, 0), (0, 1, 1), (1, 0, 0), (1, 0, 1), (1, 1, 0), (1, 1, 1)]


def corner_values(extended, size_x, size_y, size_z):
    return jnp.stack([extended[..., shift_x:shift_x + size_x, shift_y:shift_y + size_y, shift_z:shift_z + size_z] for shift_x, shift_y, shift_z in corner_list], 0)


def scatter_corners(pieces):
    leading = pieces.ndim - 4
    overall = 0.0
    for corner, (shift_x, shift_y, shift_z) in enumerate(corner_list):
        widths = [(0, 0)] * leading + [(shift_x, 1 - shift_x), (shift_y, 1 - shift_y), (shift_z, 1 - shift_z)]
        overall = overall + jnp.pad(pieces[corner], widths)
    return overall


def element_pass(extended, stiff_field, element_four):
    size_x, size_y, size_z = stiff_field.shape
    corner_vals = corner_values(extended, size_x, size_y, size_z)
    forces = jnp.einsum('adbe,bkexyz->akdxyz', element_four, corner_vals, precision=highest)
    energy_stiff = jnp.einsum('akdxyz,akdxyz->kxyz', corner_vals, forces, precision=highest)
    energy_mass = jnp.sum(corner_vals * corner_vals, axis=(0, 2)) * 0.125
    return scatter_corners(forces * stiff_field), energy_stiff, energy_mass


def stiffness_apply(block, stiff_field, free_mask, element_four):
    size_x, size_y, size_z = stiff_field.shape
    padded = jnp.pad(block, ((0, 0), (0, 0), (0, 1), (0, 1), (0, 1)))

    def single_column(column):
        assembled, energy_stiff, energy_mass = element_pass(column[None], stiff_field, element_four)
        return assembled[0], energy_stiff[0], energy_mass[0]

    assembled, energy_stiff, energy_mass = lax.map(single_column, padded)
    return assembled[:, :, :size_x, :size_y, :size_z] * free_mask, energy_stiff, energy_mass


def gram_matrix(left_blocks, right_blocks):
    gram_rows = []
    for left_block in left_blocks:
        flat_left = left_block.reshape(left_block.shape[0], -1)
        gram_rows.append(jnp.concatenate([jnp.einsum('ik,jk->ij', flat_left, right_block.reshape(right_block.shape[0], -1), precision=highest) for right_block in right_blocks], 1))
    return jnp.concatenate(gram_rows, 0)


def reference(current, previous, element_stiffness, preconditioner, modulus, density, solid, clamped):
    element_four = element_stiffness.reshape(8, 3, 8, 3)
    size_x, size_y, size_z = modulus.shape
    dof_count = 3.0 * size_x * size_y * size_z
    bottom = (jnp.arange(size_z) == 0).astype(jnp.float32)
    free_mask = 1.0 - clamped.astype(jnp.float32)[:, :, None] * bottom
    grams_stiff = []
    grams_mass = []
    searches = []
    records = []
    for realization in range(REALS):
        solid_share = solid[realization].astype(jnp.float32)
        stiff_field = modulus * (0.02 + 0.98 * solid_share)
        mass_field = density * (0.1 + 0.9 * solid_share)
        lumped = scatter_corners(jnp.stack([mass_field * 0.125] * 8, 0))[:size_x, :size_y, :size_z] * free_mask
        current_free = current[realization] * free_mask
        previous_free = previous[realization] * free_mask
        stiff_cur, energy_stiff, energy_mass = stiffness_apply(current_free, stiff_field, free_mask, element_four)
        stiff_prev, _, _ = stiffness_apply(previous_free, stiff_field, free_mask, element_four)
        mass_cur = lumped * current_free
        mass_prev = lumped * previous_free
        numerator = jnp.sum(current_free * stiff_cur, axis=(1, 2, 3, 4)) / dof_count
        denominator = jnp.sum(current_free * mass_cur, axis=(1, 2, 3, 4)) / dof_count
        quotient = numerator / denominator
        search = preconditioner[realization][None] * (stiff_cur - mass_cur * quotient[:, None, None, None, None])
        stiff_search, _, _ = stiffness_apply(search, stiff_field, free_mask, element_four)
        mass_search = lumped * search
        search_basis = [current_free, search, previous_free]
        grams_stiff.append(gram_matrix(search_basis, [stiff_cur, stiff_search, stiff_prev]) / dof_count)
        grams_mass.append(gram_matrix(search_basis, [mass_cur, mass_search, mass_prev]) / dof_count)
        searches.append(search)
        records.append((quotient, denominator, energy_stiff, energy_mass, stiff_field, mass_field))
    powered = [record[0] ** (-soft_power) for record in records]
    overall = jnp.sum(jnp.stack([jnp.sum(entry) for entry in powered]))
    sensitivity = jnp.zeros((size_x, size_y, size_z), jnp.float32)
    for entry, (quotient, denominator, energy_stiff, energy_mass, stiff_field, mass_field) in zip(powered, records):
        coefficient = entry / overall / denominator
        sensitivity = sensitivity + 3.0 * stiff_field * jnp.einsum('j,jxyz->xyz', coefficient, energy_stiff, precision=highest) - mass_field * jnp.einsum('j,jxyz->xyz', coefficient * quotient, energy_mass, precision=highest)
    return jnp.stack(grams_stiff), jnp.stack(grams_mass), jnp.stack(searches), sensitivity
```

```python
import numpy as np
import jax
import jax.numpy as jnp
from jax import lax
from jax.experimental import pallas as pl
from jax.experimental.pallas import tpu as pltpu
from jax.sharding import PartitionSpec as P

f32 = jnp.float32
bf16 = jnp.bfloat16
SLAB = 16
NODE_ROWS = 112
FORCE_ROWS = 192
EDGE = 64


def operator_tables(rows):
    row_pick = np.zeros((2, NODE_ROWS + FORCE_ROWS, 24), np.float32)
    col_pick = np.zeros((24, FORCE_ROWS + EDGE), np.float32)
    col_y = np.full(FORCE_ROWS + EDGE, -99)
    for beta in range(24):
        for y in range(rows):
            col_pick[beta, beta * rows + y] = 1
            col_y[beta * rows + y] = y
    for a in range(2):
        for q in range(2):
            for d in range(3):
                for j in range(4):
                    k = FORCE_ROWS + (a * 2 + q) * 16 + d * 4 + j
                    col_pick[(4 * a + 2 * (j % 2) + q) * 3 + d, k] = 1
                    col_y[k] = -1 if j < 2 else rows
    mask = np.zeros((2, NODE_ROWS + FORCE_ROWS, FORCE_ROWS + EDGE), np.float32)
    for q in range(2):
        for a in range(2):
            for d in range(3):
                for y in range(rows + 1):
                    m = (q * 6 + a * 3 + d) * rows + y
                    if y == rows:
                        m = 12 * rows + q * 8 + a * 3 + d
                    for b in range(2):
                        row_pick[b, m, (4 * a + 2 * b + q) * 3 + d] = 1
                        mask[b, m] = col_y == y - b
    for alpha in range(24):
        for y in range(rows):
            m = NODE_ROWS + alpha * rows + y
            row_pick[0, m, alpha] = 1
            mask[0, m, :FORCE_ROWS] = col_y[:FORCE_ROWS] == y
    return row_pick, col_pick, mask


def split(value):
    high = value.astype(bf16)
    return high, (value - high.astype(f32)).astype(bf16)


def dot(left, right):
    return jnp.dot(left, right, preferred_element_type=f32)


def operator_kernel(matrix, row_pick, col_pick, mask, high_out, low_out):
    high, low = split(matrix[...])
    for part, out in ((high, high_out), (low, low_out)):
        total = 0.0
        for b in range(2):
            picked = dot(row_pick[b], part).astype(bf16)
            total = total + dot(picked, col_pick[...]) * mask[b].astype(f32)
        out[...] = total.astype(bf16)


def prepare_kernel(sizes, cur, prev, modulus, density, solid, precond, mask, own, prev_free, up, down):
    cols, sx, sy, sz = sizes
    slabs = cols * 3
    block = slabs * sx * sy
    free = mask[...]
    share = solid[0].astype(f32)
    own[0:block] = (cur[0] * free[None, None]).reshape(block, sz)
    masked = prev[0] * free[None, None]
    prev_free[...] = masked.reshape(block, sz)
    own[block : block + slabs * sy] = masked[:, :, 0].reshape(slabs * sy, sz)
    field = block + slabs * sy
    plane = sx * sy
    own[field : field + plane] = (modulus[...] * (0.02 + 0.98 * share)).reshape(plane, sz)
    own[field + plane : field + 2 * plane] = (density[...] * (0.1 + 0.9 * share) * 0.125).reshape(plane, sz)
    own[field + 2 * plane : field + 5 * plane] = (precond[0] * free[None]).reshape(3 * plane, sz)
    n = slabs * sx
    up[0:n] = own[pl.ds(sy - 1, n, stride=sy), :]
    up[n : n + 2 * sx] = own[pl.ds(field + sy - 1, 2 * sx, stride=sy), :]
    up[n + 2 * sx :] = jnp.zeros((up.shape[0] - n - 2 * sx, sz), f32)
    down[0:n] = own[pl.ds(0, n, stride=sy), :]
    down[n : 2 * n] = own[pl.ds(1, n, stride=sy), :]
    down[2 * n : 3 * n] = prev_free[pl.ds(0, n, stride=sy), :]
    down[3 * n : 3 * n + 5 * sx] = own[pl.ds(field, 5 * sx, stride=sy), :]
    down[3 * n + 5 * sx :] = jnp.zeros((down.shape[0] - 3 * n - 5 * sx, sz), f32)


def main_kernel(
    sizes, odd, own, prev_free, from_low, from_high, pair_a, pair_b, op_high, op_low,
    gram_out, a_out, b_out, stiff_out, mass_out,
    basis, edge, applied, stiff, stiff_edge, mass_rows, lumped, scale,
):
    cols, sx, sy, sz = sizes
    slabs = cols * 3
    block = slabs * sx * sy
    plane = sx * sy
    field = block + slabs * sy
    own_rows = own.shape[0]
    low_rows = from_low.shape[0]
    width = 4 * cols
    n = slabs * sx
    layers = sx + 3

    def base(layer, k, d):
        return (((layer + 1) * width + k) * 3 + d) * SLAB

    def out_base(layer, k, d):
        return ((layer * width + k) * 3 + d) * SLAB

    lane = lax.broadcasted_iota(jnp.int32, (8, sz), 1)
    not_last = (lane < sz - 1).astype(f32)
    not_first = (lane > 0).astype(f32)

    def unpack(layer, source, low, high, at):
        low_ref, low_at = low
        high_ref, high_at = high
        for k in range(cols):
            for d in range(3):
                basis[pl.ds(base(layer, k, d), sy), :] = source[pl.ds(((k * 3 + d) * sx + at) * sy, sy), :]
        basis[pl.ds(base(layer, 0, 0) + sy, slabs, stride=SLAB), :] = high_ref[pl.ds(high_at + at, slabs, stride=sx), :]
        for d in range(3):
            start = (layer + 1) * cols * SLAB + d * 4
            pick = d * sx + at
            edge[pl.ds(start, cols, stride=SLAB), :] = low_ref[pl.ds(low_at + pick, cols, stride=3 * sx), :]
            edge[pl.ds(start + 1, cols, stride=SLAB), :] = source[pl.ds(pick * sy, cols, stride=3 * sx * sy), :]
            edge[pl.ds(start + 2, cols, stride=SLAB), :] = high_ref[pl.ds(high_at + pick, cols, stride=3 * sx), :]
            edge[pl.ds(start + 3, cols, stride=SLAB), :] = high_ref[pl.ds(high_at + n + pick, cols, stride=3 * sx), :]

    def unpack_fields(layer, source, low, high, at):
        low_ref, low_at = low
        high_ref, high_at = high
        index = layer + 1
        stiff[pl.ds(index * sy, sy), :] = source[pl.ds(field + at * sy, sy), :]
        before = low_ref[pl.ds(low_at + n + at, 1), :]
        after = high_ref[pl.ds(high_at + 3 * n + at, 1), :]
        for j in range(4):
            row = before if j < 2 else after
            stiff_edge[pl.ds(index * SLAB + j, 3, stride=4), :] = jnp.broadcast_to(row, (3, sz))
        mass_rows[pl.ds(index * SLAB, 1), :] = low_ref[pl.ds(low_at + n + sx + at, 1), :]
        mass_rows[pl.ds(index * SLAB + 1, sy), :] = source[pl.ds(field + plane + at * sy, sy), :]
        mass_rows[pl.ds(index * SLAB + 1 + sy, 1), :] = high_ref[pl.ds(high_at + 3 * n + sx + at, 1), :]

    def unpack_nodes(layer, source, prev_source, high, at, prev_stride, prev_at):
        high_ref, high_at = high
        for k in range(cols):
            for d in range(3):
                basis[pl.ds(base(layer, 3 * cols + k, d), sy), :] = prev_source[
                    pl.ds(prev_at + ((k * 3 + d) * prev_stride) * sy, sy), :
                ]
        basis[pl.ds(base(layer, 3 * cols, 0) + sy, slabs, stride=SLAB), :] = high_ref[
            pl.ds(high_at + 2 * n + at, slabs, stride=sx), :
        ]
        for d in range(3):
            scale[pl.ds((layer * 3 + d) * SLAB, sy), :] = source[pl.ds(field + 2 * plane + (d * sx + at) * sy, sy), :]
        scale[pl.ds(layer * 3 * SLAB + sy, 3, stride=SLAB), :] = high_ref[pl.ds(high_at + 3 * n + 2 * sx + at, 3, stride=sx), :]

    edge[...] = jnp.zeros(edge.shape, f32)
    stiff_edge[...] = jnp.zeros(stiff_edge.shape, f32)
    own_low = (from_low, 0)
    own_high = (from_high, 0)
    for layer in range(sx):
        unpack(layer, own, own_low, own_high, layer)
        unpack_fields(layer, own, own_low, own_high, layer)
        unpack_nodes(layer, own, prev_free, own_high, layer, sx, layer * sy)

    def unpack_sides(lower, upper):
        low_at = own_rows
        high_at = own_rows + low_rows
        unpack(-1, lower, (lower, low_at), (lower, high_at), sx - 1)
        unpack_fields(-1, lower, (lower, low_at), (lower, high_at), sx - 1)
        for step in range(2):
            unpack(sx + step, upper, (upper, low_at), (upper, high_at), step)
        unpack_fields(sx, upper, (upper, low_at), (upper, high_at), 0)
        unpack_nodes(sx, upper, upper, (upper, high_at), 0, 1, block)

    @pl.when(odd[0] == 1)
    def _():
        unpack_sides(pair_a, pair_b)

    @pl.when(odd[0] == 0)
    def _():
        unpack_sides(pair_b, pair_a)

    for layer in range(sx + 1):
        first = layer * SLAB
        second = first + SLAB
        mass_sum = mass_rows[pl.ds(first, SLAB), :] + mass_rows[pl.ds(second, SLAB), :]
        lumped[pl.ds(layer * SLAB, SLAB), :] = mass_sum
        inner = lumped[pl.ds(layer * SLAB, sy), :] + lumped[pl.ds(layer * SLAB + 1, sy), :]
        outer = lumped[pl.ds(layer * SLAB + sy, 1), :] + lumped[pl.ds(layer * SLAB + sy + 1, 1), :]
        lumped[pl.ds(layer * SLAB, sy), :] = inner + pltpu.roll(inner, 1, 1) * not_first
        outer = jnp.broadcast_to(outer, (8, sz))
        outer = outer + pltpu.roll(outer, 1, 1) * not_first
        lumped[pl.ds(layer * SLAB + sy, 1), :] = outer[0:1]

    def corner_tiles(k, layer):
        tiles = []
        for a in range(2):
            for b in range(2):
                near = [basis[pl.ds(base(layer + a, k, d) + b, sy), :] for d in range(3)]
                tiles += near
                tiles += [pltpu.roll(tile, sz - 1, 1) for tile in near]
        return tiles

    def weights(layer):
        plain = stiff[pl.ds((layer + 1) * sy, sy), :]
        return plain, plain * not_last

    def scaled(tiles, layer):
        plain, cut = weights(layer)
        return [tile * (cut if (i // 3) % 2 else plain) for i, tile in enumerate(tiles)]

    def edge_tiles(k, layer):
        plain = stiff_edge[pl.ds((layer + 1) * SLAB, SLAB), :]
        cut = plain * jnp.concatenate([not_last, not_last], 0)
        tiles = []
        for a in range(2):
            tile = edge[pl.ds(((layer + 1 + a) * cols + k) * SLAB, SLAB), :]
            tiles.append(tile * plain)
            tiles.append(pltpu.roll(tile, sz - 1, 1) * cut)
        return tiles

    def apply(columns, rows, depth):
        high, low = split(jnp.concatenate(columns, 1))
        return (
            dot(op_high[0:rows, 0:depth], high)
            + dot(op_low[0:rows, 0:depth], high)
            + dot(op_high[0:rows, 0:depth], low)
        )

    def node_parts(out):
        parts = []
        for i in range(6):
            shifted = pltpu.roll(out[(6 + i) * sy : (7 + i) * sy], 1, 1) * not_first
            parts.append(out[i * sy : (i + 1) * sy] + shifted)
        rim = out[12 * sy : 12 * sy + 8] + pltpu.roll(out[12 * sy + 8 : 12 * sy + 16], 1, 1) * not_first
        return parts, rim

    def current_pair(pair, carry):
        tails = [None, None]
        for layer in range(-1, sx + 1):
            inner = 0 <= layer < sx
            columns = []
            kept = []
            for c in range(2):
                k = pair * 2 + c
                tiles = corner_tiles(k, layer)
                kept.append(tiles)
                columns.append(jnp.concatenate(scaled(tiles, layer) + edge_tiles(k, layer), 0))
            out = apply(columns, NODE_ROWS + FORCE_ROWS if inner else NODE_ROWS, FORCE_ROWS + EDGE)
            for c in range(2):
                k = pair * 2 + c
                part = out[:, c * sz : (c + 1) * sz]
                if inner:
                    energy = [0.0, 0.0]
                    square = [0.0, 0.0]
                    for alpha in range(24):
                        q = (alpha // 3) % 2
                        tile = kept[c][alpha]
                        energy[q] = energy[q] + tile * part[NODE_ROWS + alpha * sy : NODE_ROWS + (alpha + 1) * sy]
                        square[q] = square[q] + tile * tile
                    at = (k * sx + layer) * sy
                    mass = mass_rows[pl.ds((layer + 1) * SLAB + 1, sy), :]
                    stiff_out[pl.ds(at, sy), :] = 3.0 * (energy[0] + energy[1] * not_last)
                    mass_out[pl.ds(at, sy), :] = mass * (square[0] + square[1] * not_last)
                parts, rim = node_parts(part)
                if layer >= 0:
                    before, rim_before = tails[c]
                    rim_sum = rim[0:3] + rim_before[3:6]
                    load = lumped[pl.ds(layer * SLAB, SLAB), :]
                    for d in range(3):
                        total = parts[d] + before[3 + d]
                        factor = scale[pl.ds((layer * 3 + d) * SLAB, SLAB), :]
                        a_value = factor[0:sy] * total
                        b_value = factor * load * basis[pl.ds(base(layer, k, d), SLAB), :]
                        basis[pl.ds(base(layer, cols + k, d), sy), :] = a_value
                        basis[pl.ds(base(layer, cols + k, d) + sy, 1), :] = factor[sy : sy + 1] * rim_sum[d : d + 1]
                        basis[pl.ds(base(layer, 2 * cols + k, d), SLAB), :] = b_value
                        if layer < sx:
                            applied[pl.ds(out_base(layer, k, d), sy), :] = total
                            at = ((k * 3 + d) * sx + layer) * sy
                            a_out[pl.ds(at, sy), :] = a_value
                            b_out[pl.ds(at, sy), :] = b_value[0:sy]
                        else:
                            applied[pl.ds(out_base(layer, k, d), sy), :] = jnp.zeros((sy, sz), f32)
                        applied[pl.ds(out_base(layer, k, d) + sy, 1), :] = jnp.zeros((1, sz), f32)
                tails[c] = (parts, rim)
        return carry

    lax.fori_loop(0, cols // 2, current_pair, 0)

    def other_pair(pair, carry):
        tails = [None, None]
        for layer in range(sx):
            columns = []
            for c in range(2):
                k = cols + pair * 2 + c
                columns.append(jnp.concatenate(scaled(corner_tiles(k, layer), layer), 0))
            out = apply(columns, NODE_ROWS, FORCE_ROWS)
            for c in range(2):
                k = cols + pair * 2 + c
                parts, rim = node_parts(out[:, c * sz : (c + 1) * sz])
                ends = [(layer, parts[0:3], rim[0:3], tails[c])]
                if layer == sx - 1:
                    ends.append((sx, parts[3:6], rim[3:6], None))
                for at, values, row, before in ends:
                    for d in range(3):
                        value = values[d]
                        last = row[d : d + 1]
                        if before is not None:
                            value = value + before[0][3 + d]
                            last = last + before[1][3 + d : 4 + d]
                        applied[pl.ds(out_base(at, k, d), sy), :] = value
                        applied[pl.ds(out_base(at, k, d) + sy, 1), :] = last
                tails[c] = (parts, rim)
        return carry

    lax.fori_loop(0, 3 * cols // 2, other_pair, 0)

    def stacked(values):
        high, low = split(jnp.concatenate(values, 1))
        return high, low

    def contract(left, right):
        return lax.dot_general(left, right, (((1,), (1,)), ((), ())), preferred_element_type=f32)

    step = 3 * SLAB

    def product(left_values, right_values):
        left_high, left_low = stacked(left_values)
        right_high, right_low = stacked(right_values)
        return contract(left_high, right_high) + contract(left_high, right_low) + contract(left_low, right_high)

    def gram_group(index, carry):
        layer = index // 3
        d = index - layer * 3
        left = []
        right = []
        right_mass = []
        for y in range(sy):
            value = basis[pl.ds(((layer + 1) * width * 3 + d) * SLAB + y, width, stride=step), :]
            left.append(value)
            right.append(applied[pl.ds((layer * width * 3 + d) * SLAB + y, width, stride=step), :])
            right_mass.append(value * lumped[pl.ds(layer * SLAB + y, 1), :])
        left_high, left_low = stacked(left)
        right_all = [jnp.concatenate([x, z], 0) for x, z in zip(right, right_mass)]
        right_high, right_low = stacked(right_all)
        return carry + contract(left_high, right_high) + contract(left_high, right_low) + contract(left_low, right_high)

    both = lax.fori_loop(0, 3 * sx, gram_group, jnp.zeros((width, 2 * width), f32))
    gram_stiff = both[:, 0:width]
    for d in range(3):
        left = []
        right = []
        for y in range(sy):
            left.append(basis[pl.ds(base(sx, 0, d) + y, width, stride=step), :])
            right.append(applied[pl.ds(out_base(sx, 0, d) + y, width, stride=step), :])
        gram_stiff = gram_stiff + product(left, right)
    left = []
    right = []
    for layer in range(sx + 1):
        for d in range(3):
            left.append(basis[pl.ds(base(layer, 0, d) + sy, width, stride=step), :])
            right.append(applied[pl.ds(out_base(layer, 0, d) + sy, width, stride=step), :])
    gram_stiff = gram_stiff + product(left, right)
    gram_out[...] = jnp.zeros(gram_out.shape, f32)
    gram_out[:, 0:width] = gram_stiff
    gram_out[:, 64 : 64 + width] = both[:, width : 2 * width]


def finish_kernel(sizes, dof, gram, a_in, b_in, stiff_in, mass_in, stiff_gram, mass_gram, search, terms):
    cols, sx, sy, sz = sizes
    eye = (
        lax.broadcasted_iota(jnp.int32, (cols, cols), 0) == lax.broadcasted_iota(jnp.int32, (cols, cols), 1)
    ).astype(f32)
    top = gram[0:cols, 0:cols] * eye
    bottom = gram[0:cols, 64 : 64 + cols] * eye
    quotient = jnp.sum(top, 1, keepdims=True) / jnp.sum(bottom, 1, keepdims=True)
    quotient_row = jnp.sum(top, 0, keepdims=True) / jnp.sum(bottom, 0, keepdims=True)
    for at, out in ((0, stiff_gram), (64, mass_gram)):
        whole = gram[:, at : at + 4 * cols]
        rows = jnp.concatenate(
            [whole[0:cols], whole[cols : 2 * cols] - quotient * whole[2 * cols : 3 * cols], whole[3 * cols :]], 0
        )
        out[0] = (1.0 / dof) * jnp.concatenate(
            [
                rows[:, 0:cols],
                rows[:, cols : 2 * cols] - quotient_row * rows[:, 2 * cols : 3 * cols],
                rows[:, 3 * cols :],
            ],
            1,
        )
    squared = quotient * quotient
    powered = 1.0 / (squared * squared)
    coefficient = powered / (jnp.sum(bottom, 1, keepdims=True) * (1.0 / dof))
    weighted = coefficient * quotient
    plane = sx * sy
    total = 0.0
    for j in range(cols):
        here = pl.ds(j * 3 * plane, 3 * plane)
        value = a_in[here, :] - quotient[j : j + 1] * b_in[here, :]
        search[0, j] = value.reshape(3, sx, sy, sz)
        part = pl.ds(j * plane, plane)
        total = total + coefficient[j : j + 1] * stiff_in[part, :] - weighted[j : j + 1] * mass_in[part, :]
    terms[0:plane] = total
    terms[plane : plane + 8] = jnp.broadcast_to(jnp.sum(powered, 0, keepdims=True), (8, sz))


def line(axis, step):
    count = lax.axis_size(axis)
    return [(i, i + step) for i in range(count) if 0 <= i + step < count]


def pairs(axis, first):
    count = lax.axis_size(axis)
    steps = []
    for i in range(first, count - 1, 2):
        steps += [(i, i + 1), (i + 1, i)]
    return steps


def sum_over(value, axis):
    count = lax.axis_size(axis)
    if count & (count - 1):
        return lax.psum(value, axis)
    distance = 1
    while distance < count:
        value = value + lax.ppermute(value, axis, [(i, i ^ distance) for i in range(count)])
        distance *= 2
    return value


def shards(current, previous, element_stiffness, preconditioner, modulus, density, solid, clamped):
    cols = current.shape[1]
    sx, sy, sz = modulus.shape
    sizes = (cols, sx, sy, sz)
    slabs = cols * 3
    n = slabs * sx
    block = n * sy
    dof = 3.0 * sx * sy * sz * lax.axis_size("bx") * lax.axis_size("by")
    bottom = (jnp.arange(sz) == 0).astype(f32)
    mask = 1.0 - clamped.astype(f32)[:, :, None] * bottom

    def struct(*shape, dtype=f32):
        return jax.ShapeDtypeStruct(shape, dtype)

    own_rows = block + slabs * sy + 5 * sx * sy
    up_rows = -(-(n + 2 * sx) // 8) * 8
    down_rows = -(-(3 * n + 5 * sx) // 8) * 8
    own, prev_free, up, down = pl.pallas_call(
        lambda *refs: prepare_kernel(sizes, *refs),
        out_shape=(struct(own_rows, sz), struct(block, sz), struct(up_rows, sz), struct(down_rows, sz)),
        name="prepare",
    )(current, previous, modulus, density, solid, preconditioner, mask)
    from_low = lax.ppermute(up, "by", line("by", 1))
    from_high = lax.ppermute(down, "by", line("by", -1))
    row_pick, col_pick, op_mask = operator_tables(sy)
    op_high, op_low = pl.pallas_call(
        operator_kernel,
        out_shape=(struct(NODE_ROWS + FORCE_ROWS, FORCE_ROWS + EDGE, dtype=bf16),) * 2,
        name="operator",
    )(element_stiffness, jnp.asarray(row_pick, bf16), jnp.asarray(col_pick, bf16), jnp.asarray(op_mask, bf16))
    message = jnp.concatenate([own, from_low, from_high], 0)
    pair_a = lax.ppermute(message, "bx", pairs("bx", 0))
    pair_b = lax.ppermute(message, "bx", pairs("bx", 1))
    odd = (lax.axis_index("bx") % 2).astype(jnp.int32).reshape(1)
    width = 4 * cols
    vmem = pl.BlockSpec(memory_space=pltpu.VMEM)
    gram, a_part, b_part, stiff_part, mass_part = pl.pallas_call(
        lambda *refs: main_kernel(sizes, *refs),
        in_specs=[pl.BlockSpec(memory_space=pltpu.SMEM)] + [vmem] * 8,
        out_shape=(
            struct(width, 128),
            struct(block, sz),
            struct(block, sz),
            struct(cols * sx * sy, sz),
            struct(cols * sx * sy, sz),
        ),
        scratch_shapes=[
            pltpu.VMEM(((sx + 3) * width * 3 * SLAB, sz), f32),
            pltpu.VMEM(((sx + 3) * cols * SLAB, sz), f32),
            pltpu.VMEM(((sx + 1) * width * 3 * SLAB, sz), f32),
            pltpu.VMEM(((sx + 2) * sy, sz), f32),
            pltpu.VMEM(((sx + 2) * SLAB, sz), f32),
            pltpu.VMEM(((sx + 2) * SLAB, sz), f32),
            pltpu.VMEM(((sx + 1) * SLAB, sz), f32),
            pltpu.VMEM(((sx + 1) * 3 * SLAB, sz), f32),
        ],
        name="main",
    )(odd, own, prev_free, from_low, from_high, pair_a, pair_b, op_high, op_low)
    gram = sum_over(sum_over(gram, "bx"), "by")
    stiff_gram, mass_gram, search, terms = pl.pallas_call(
        lambda *refs: finish_kernel(sizes, dof, *refs),
        out_shape=(
            struct(1, 3 * cols, 3 * cols),
            struct(1, 3 * cols, 3 * cols),
            struct(1, cols, 3, sx, sy, sz),
            struct(sx * sy + 8, sz),
        ),
        name="finish",
    )(gram, a_part, b_part, stiff_part, mass_part)
    terms = sum_over(terms, "real")
    share = sz // lax.axis_size("real")
    plane = sx * sy
    mine = lax.dynamic_slice_in_dim(terms[:plane], lax.axis_index("real") * share, share, 1)
    sensitivity = (mine / terms[plane:, :1][:1]).reshape(sx, sy, share)
    return stiff_gram, mass_gram, search, sensitivity


def solution(mesh):
    in_specs = (
        P("real", None, None, "bx", "by", None),
        P("real", None, None, "bx", "by", None),
        P(),
        P("real", None, "bx", "by", None),
        P("bx", "by", None),
        P("bx", "by", None),
        P("real", "bx", "by", None),
        P("bx", "by"),
    )
    out_specs = (
        P("real", None, None),
        P("real", None, None),
        P("real", None, None, "bx", "by", None),
        P("bx", "by", "real"),
    )
    return jax.shard_map(shards, mesh=mesh, in_specs=in_specs, out_specs=out_specs, check_vma=False)
```

```python
import numpy as np
import jax
import jax.numpy as jnp
from jax import lax
from jax.experimental import pallas as pl
from jax.experimental.pallas import tpu as pltpu
from jax.sharding import PartitionSpec as P

f32 = jnp.float32
bf16 = jnp.bfloat16
SLAB = 16
NODE_ROWS = 112
FORCE_ROWS = 192
EDGE = 64


def operator_tables(rows):
    row_pick = np.zeros((2, NODE_ROWS + FORCE_ROWS, 24), np.float32)
    col_pick = np.zeros((24, FORCE_ROWS + EDGE), np.float32)
    col_y = np.full(FORCE_ROWS + EDGE, -99)
    for beta in range(24):
        for y in range(rows):
            col_pick[beta, beta * rows + y] = 1
            col_y[beta * rows + y] = y
    for a in range(2):
        for q in range(2):
            for d in range(3):
                for j in range(4):
                    k = FORCE_ROWS + (a * 2 + q) * 16 + d * 4 + j
                    col_pick[(4 * a + 2 * (j % 2) + q) * 3 + d, k] = 1
                    col_y[k] = -1 if j < 2 else rows
    mask = np.zeros((2, NODE_ROWS + FORCE_ROWS, FORCE_ROWS + EDGE), np.float32)
    for q in range(2):
        for a in range(2):
            for d in range(3):
                for y in range(rows + 1):
                    m = (q * 6 + a * 3 + d) * rows + y
                    if y == rows:
                        m = 12 * rows + q * 8 + a * 3 + d
                    for b in range(2):
                        row_pick[b, m, (4 * a + 2 * b + q) * 3 + d] = 1
                        mask[b, m] = col_y == y - b
    for alpha in range(24):
        for y in range(rows):
            m = NODE_ROWS + alpha * rows + y
            row_pick[0, m, alpha] = 1
            mask[0, m, :FORCE_ROWS] = col_y[:FORCE_ROWS] == y
    return row_pick, col_pick, mask


def split(value):
    high = value.astype(bf16)
    return high, (value - high.astype(f32)).astype(bf16)


def dot(left, right):
    return jnp.dot(left, right, preferred_element_type=f32)


def operator_kernel(matrix, row_pick, col_pick, mask, high_out, low_out):
    high, low = split(matrix[...])
    for part, out in ((high, high_out), (low, low_out)):
        total = 0.0
        for b in range(2):
            picked = dot(row_pick[b], part).astype(bf16)
            total = total + dot(picked, col_pick[...]) * mask[b].astype(f32)
        out[...] = total.astype(bf16)


def prepare_kernel(sizes, *refs):
    sources = refs[0:7]
    own, prev_free, up, down = refs[7:11]
    buffers = refs[11:18]
    arrived = refs[18]
    copies = [pltpu.make_async_copy(source, buffer, arrived.at[i]) for i, (source, buffer) in enumerate(zip(sources, buffers))]
    for copy in copies:
        copy.start()
    for copy in copies:
        copy.wait()
    cur, prev, modulus, density, solid, precond, clamped = buffers
    cols, sx, sy, sz = sizes
    slabs = cols * 3
    block = slabs * sx * sy
    held = clamped[...].astype(f32)
    eye = (lax.broadcasted_iota(jnp.int32, (sy, sy), 0) == lax.broadcasted_iota(jnp.int32, (sy, sy), 1)).astype(f32)
    bottom = (lax.broadcasted_iota(jnp.int32, (sy, sz), 1) == 0).astype(f32)
    planes = []
    for x in range(sx):
        column = jnp.sum(jnp.broadcast_to(held[x : x + 1], (sy, sy)) * eye, 1, keepdims=True)
        planes.append((1.0 - column * bottom)[None])
    free = jnp.concatenate(planes, 0)
    share = solid[0].astype(f32)
    own[0:block] = (cur[0] * free[None, None]).reshape(block, sz)
    masked = prev[0] * free[None, None]
    prev_free[...] = masked.reshape(block, sz)
    own[block : block + slabs * sy] = masked[:, :, 0].reshape(slabs * sy, sz)
    field = block + slabs * sy
    plane = sx * sy
    own[field : field + plane] = (modulus[...] * (0.02 + 0.98 * share)).reshape(plane, sz)
    own[field + plane : field + 2 * plane] = (density[...] * (0.1 + 0.9 * share) * 0.125).reshape(plane, sz)
    own[field + 2 * plane : field + 5 * plane] = (precond[0] * free[None]).reshape(3 * plane, sz)
    n = slabs * sx
    up[0:n] = own[pl.ds(sy - 1, n, stride=sy), :]
    up[n : n + 2 * sx] = own[pl.ds(field + sy - 1, 2 * sx, stride=sy), :]
    up[n + 2 * sx :] = jnp.zeros((up.shape[0] - n - 2 * sx, sz), f32)
    down[0:n] = own[pl.ds(0, n, stride=sy), :]
    down[n : 2 * n] = own[pl.ds(1, n, stride=sy), :]
    down[2 * n : 3 * n] = prev_free[pl.ds(0, n, stride=sy), :]
    down[3 * n : 3 * n + 5 * sx] = own[pl.ds(field, 5 * sx, stride=sy), :]
    down[3 * n + 5 * sx :] = jnp.zeros((down.shape[0] - 3 * n - 5 * sx, sz), f32)


def main_kernel(
    sizes, odd, own, prev_free, from_low, from_high,
    pair_a, pair_b, corner_a, corner_b, op_high, op_low,
    gram_out, a_out, b_out, stiff_out, mass_out,
    basis, edge, applied, stiff, stiff_edge, mass_rows, lumped, scale,
):
    cols, sx, sy, sz = sizes
    slabs = cols * 3
    block = slabs * sx * sy
    plane = sx * sy
    field = block + slabs * sy
    low_rows = from_low.shape[0]
    width = 4 * cols
    n = slabs * sx
    span = sy + 1

    def base(layer, k, d):
        return (((layer + 1) * width + k) * 3 + d) * span

    def out_base(layer, k, d):
        return ((layer * width + k) * 3 + d) * span

    lane = lax.broadcasted_iota(jnp.int32, (8, sz), 1)
    not_last = (lane < sz - 1).astype(f32)
    not_first = (lane > 0).astype(f32)

    def unpack(layer, source, low, high, at):
        low_ref, low_at = low
        high_ref, high_at = high
        for k in range(cols):
            for d in range(3):
                basis[pl.ds(base(layer, k, d), sy), :] = source[pl.ds(((k * 3 + d) * sx + at) * sy, sy), :]
        basis[pl.ds(base(layer, 0, 0) + sy, slabs, stride=span), :] = high_ref[pl.ds(high_at + at, slabs, stride=sx), :]
        for d in range(3):
            start = (layer + 1) * cols * SLAB + d * 4
            pick = d * sx + at
            edge[pl.ds(start, cols, stride=SLAB), :] = low_ref[pl.ds(low_at + pick, cols, stride=3 * sx), :]
            edge[pl.ds(start + 1, cols, stride=SLAB), :] = source[pl.ds(pick * sy, cols, stride=3 * sx * sy), :]
            edge[pl.ds(start + 2, cols, stride=SLAB), :] = high_ref[pl.ds(high_at + pick, cols, stride=3 * sx), :]
            edge[pl.ds(start + 3, cols, stride=SLAB), :] = high_ref[pl.ds(high_at + n + pick, cols, stride=3 * sx), :]

    def unpack_fields(layer, source, low, high, at):
        low_ref, low_at = low
        high_ref, high_at = high
        index = layer + 1
        stiff[pl.ds(index * sy, sy), :] = source[pl.ds(field + at * sy, sy), :]
        before = low_ref[pl.ds(low_at + n + at, 1), :]
        after = high_ref[pl.ds(high_at + 3 * n + at, 1), :]
        for j in range(4):
            row = before if j < 2 else after
            stiff_edge[pl.ds(index * SLAB + j, 3, stride=4), :] = jnp.broadcast_to(row, (3, sz))
        mass_rows[pl.ds(index * SLAB, 1), :] = low_ref[pl.ds(low_at + n + sx + at, 1), :]
        mass_rows[pl.ds(index * SLAB + 1, sy), :] = source[pl.ds(field + plane + at * sy, sy), :]
        mass_rows[pl.ds(index * SLAB + 1 + sy, 1), :] = high_ref[pl.ds(high_at + 3 * n + sx + at, 1), :]

    def unpack_nodes(layer, source, prev_source, high, at, prev_stride, prev_at):
        high_ref, high_at = high
        for k in range(cols):
            for d in range(3):
                basis[pl.ds(base(layer, 3 * cols + k, d), sy), :] = prev_source[
                    pl.ds(prev_at + ((k * 3 + d) * prev_stride) * sy, sy), :
                ]
        basis[pl.ds(base(layer, 3 * cols, 0) + sy, slabs, stride=span), :] = high_ref[
            pl.ds(high_at + 2 * n + at, slabs, stride=sx), :
        ]
        for d in range(3):
            scale[pl.ds((layer * 3 + d) * SLAB, sy), :] = source[pl.ds(field + 2 * plane + (d * sx + at) * sy, sy), :]
        scale[pl.ds(layer * 3 * SLAB + sy, 3, stride=SLAB), :] = high_ref[pl.ds(high_at + 3 * n + 2 * sx + at, 3, stride=sx), :]

    edge[...] = jnp.zeros(edge.shape, f32)
    stiff_edge[...] = jnp.zeros(stiff_edge.shape, f32)
    own_low = (from_low, 0)
    own_high = (from_high, 0)
    for layer in range(sx):
        unpack(layer, own, own_low, own_high, layer)
        unpack_fields(layer, own, own_low, own_high, layer)
        unpack_nodes(layer, own, prev_free, own_high, layer, sx, layer * sy)

    def unpack_sides(lower, lower_corner, upper, upper_corner):
        lower_high = (lower_corner, low_rows)
        unpack(-1, lower, (lower_corner, 0), lower_high, sx - 1)
        unpack_fields(-1, lower, (lower_corner, 0), lower_high, sx - 1)
        upper_high = (upper_corner, low_rows)
        for step in range(2):
            unpack(sx + step, upper, (upper_corner, 0), upper_high, step)
        unpack_fields(sx, upper, (upper_corner, 0), upper_high, 0)
        unpack_nodes(sx, upper, upper, upper_high, 0, 1, block)

    @pl.when(odd[0] == 1)
    def _():
        unpack_sides(pair_a, corner_a, pair_b, corner_b)

    @pl.when(odd[0] == 0)
    def _():
        unpack_sides(pair_b, corner_b, pair_a, corner_a)

    for layer in range(sx + 1):
        first = layer * SLAB
        second = first + SLAB
        mass_sum = mass_rows[pl.ds(first, SLAB), :] + mass_rows[pl.ds(second, SLAB), :]
        lumped[pl.ds(layer * SLAB, SLAB), :] = mass_sum
        inner = lumped[pl.ds(layer * SLAB, sy), :] + lumped[pl.ds(layer * SLAB + 1, sy), :]
        outer = lumped[pl.ds(layer * SLAB + sy, 1), :] + lumped[pl.ds(layer * SLAB + sy + 1, 1), :]
        lumped[pl.ds(layer * SLAB, sy), :] = inner + pltpu.roll(inner, 1, 1) * not_first
        outer = jnp.broadcast_to(outer, (8, sz))
        outer = outer + pltpu.roll(outer, 1, 1) * not_first
        lumped[pl.ds(layer * SLAB + sy, 1), :] = outer[0:1]

    def corner_tiles(k, layer):
        tiles = []
        for a in range(2):
            for b in range(2):
                near = [basis[pl.ds(base(layer + a, k, d) + b, sy), :] for d in range(3)]
                tiles += near
                tiles += [pltpu.roll(tile, sz - 1, 1) for tile in near]
        return tiles

    def weights(layer):
        plain = stiff[pl.ds((layer + 1) * sy, sy), :]
        return plain, plain * not_last

    def scaled(tiles, layer):
        plain, cut = weights(layer)
        return [tile * (cut if (i // 3) % 2 else plain) for i, tile in enumerate(tiles)]

    def edge_tiles(k, layer):
        plain = stiff_edge[pl.ds((layer + 1) * SLAB, SLAB), :]
        cut = plain * jnp.concatenate([not_last, not_last], 0)
        tiles = []
        for a in range(2):
            tile = edge[pl.ds(((layer + 1 + a) * cols + k) * SLAB, SLAB), :]
            tiles.append(tile * plain)
            tiles.append(pltpu.roll(tile, sz - 1, 1) * cut)
        return tiles

    def apply(columns, rows, depth):
        value = jnp.concatenate(columns, 1)
        high = value.astype(bf16)
        rest = value - high.astype(f32)
        both = dot(jnp.concatenate([op_high[0:rows, 0:depth], op_low[0:rows, 0:depth]], 0), high)
        total = both[0:rows] + both[rows:]
        nodes = total[0:NODE_ROWS] + dot(op_high[0:NODE_ROWS, 0:depth], rest.astype(bf16))
        return nodes, total[NODE_ROWS:], value[0:FORCE_ROWS] + rest[0:FORCE_ROWS]

    def node_parts(out):
        parts = []
        for i in range(6):
            shifted = pltpu.roll(out[(6 + i) * sy : (7 + i) * sy], 1, 1) * not_first
            parts.append(out[i * sy : (i + 1) * sy] + shifted)
        rim = out[12 * sy : 12 * sy + 8] + pltpu.roll(out[12 * sy + 8 : 12 * sy + 16], 1, 1) * not_first
        return parts, rim

    def current_pair(pair, carry):
        tails = [None, None]
        for layer in range(-1, sx + 1):
            inner = 0 <= layer < sx
            columns = []
            kept = []
            for c in range(2):
                k = pair * 2 + c
                tiles = corner_tiles(k, layer)
                kept.append(tiles)
                columns.append(jnp.concatenate(scaled(tiles, layer) + edge_tiles(k, layer), 0))
            out, forces, doubled = apply(columns, NODE_ROWS + FORCE_ROWS if inner else NODE_ROWS, FORCE_ROWS + EDGE)
            for c in range(2):
                k = pair * 2 + c
                part = out[:, c * sz : (c + 1) * sz]
                if inner:
                    work = forces[:, c * sz : (c + 1) * sz] * doubled[:, c * sz : (c + 1) * sz]
                    energy = 0.0
                    square = [0.0, 0.0]
                    for alpha in range(24):
                        q = (alpha // 3) % 2
                        tile = kept[c][alpha]
                        energy = energy + work[alpha * sy : (alpha + 1) * sy]
                        square[q] = square[q] + tile * tile
                    at = (k * sx + layer) * sy
                    mass = mass_rows[pl.ds((layer + 1) * SLAB + 1, sy), :]
                    stiff_out[pl.ds(at, sy), :] = energy * (3.0 / weights(layer)[0])
                    mass_out[pl.ds(at, sy), :] = mass * (square[0] + square[1] * not_last)
                parts, rim = node_parts(part)
                if layer >= 0:
                    before, rim_before = tails[c]
                    rim_sum = rim[0:3] + rim_before[3:6]
                    load = lumped[pl.ds(layer * SLAB, SLAB), :]
                    for d in range(3):
                        total = parts[d] + before[3 + d]
                        factor = scale[pl.ds((layer * 3 + d) * SLAB, SLAB), :]
                        a_value = factor[0:sy] * total
                        both = factor * load
                        b_value = both[0:sy] * basis[pl.ds(base(layer, k, d), sy), :]
                        b_rim = both[sy : sy + 1] * basis[pl.ds(base(layer, k, d) + sy, 1), :]
                        basis[pl.ds(base(layer, cols + k, d), sy), :] = a_value
                        basis[pl.ds(base(layer, cols + k, d) + sy, 1), :] = factor[sy : sy + 1] * rim_sum[d : d + 1]
                        basis[pl.ds(base(layer, 2 * cols + k, d), sy), :] = b_value
                        basis[pl.ds(base(layer, 2 * cols + k, d) + sy, 1), :] = b_rim
                        if layer < sx:
                            applied[pl.ds(out_base(layer, k, d), sy), :] = total
                            at = ((k * 3 + d) * sx + layer) * sy
                            a_out[pl.ds(at, sy), :] = a_value
                            b_out[pl.ds(at, sy), :] = b_value
                        else:
                            applied[pl.ds(out_base(layer, k, d), sy), :] = jnp.zeros((sy, sz), f32)
                        applied[pl.ds(out_base(layer, k, d) + sy, 1), :] = jnp.zeros((1, sz), f32)
                tails[c] = (parts, rim)
        return carry

    lax.fori_loop(0, cols // 2, current_pair, 0, unroll=cols // 2)

    def other_pair(pair, carry):
        tails = [None, None]
        for layer in range(sx):
            columns = []
            for c in range(2):
                k = cols + pair * 2 + c
                columns.append(jnp.concatenate(scaled(corner_tiles(k, layer), layer), 0))
            out = apply(columns, NODE_ROWS, FORCE_ROWS)[0]
            for c in range(2):
                k = cols + pair * 2 + c
                parts, rim = node_parts(out[:, c * sz : (c + 1) * sz])
                ends = [(layer, parts[0:3], rim[0:3], tails[c])]
                if layer == sx - 1:
                    ends.append((sx, parts[3:6], rim[3:6], None))
                for at, values, row, before in ends:
                    for d in range(3):
                        value = values[d]
                        last = row[d : d + 1]
                        if before is not None:
                            value = value + before[0][3 + d]
                            last = last + before[1][3 + d : 4 + d]
                        applied[pl.ds(out_base(at, k, d), sy), :] = value
                        applied[pl.ds(out_base(at, k, d) + sy, 1), :] = last
                tails[c] = (parts, rim)
        return carry

    lax.fori_loop(0, 3 * cols // 2, other_pair, 0, unroll=3 * cols // 2)

    def contract(left, right):
        return lax.dot_general(left, right, (((1,), (1,)), ((), ())), preferred_element_type=f32)

    step = 3 * span

    def product(applied_values, basis_values):
        left_high, left_low = split(jnp.concatenate(basis_values, 1))
        right_high, right_low = split(jnp.concatenate(applied_values, 1))
        rows = left_high.shape[0]
        both = contract(jnp.concatenate([left_high, left_low], 0), right_high)
        return both[0:rows] + both[rows:] + contract(left_high, right_low)

    def gram_group(index, carry):
        layer = index // 3
        d = index - layer * 3
        values = []
        others = []
        for y in range(sy):
            value = basis[pl.ds(((layer + 1) * width * 3 + d) * span + y, width, stride=step), :]
            other = applied[pl.ds((layer * width * 3 + d) * span + y, width, stride=step), :]
            values.append(value)
            others.append(jnp.concatenate([other, value * lumped[pl.ds(layer * SLAB + y, 1), :]], 0))
        return carry + product(others, values)

    both = lax.fori_loop(0, 3 * sx, gram_group, jnp.zeros((width, 2 * width), f32))

    def gram_end(d, carry):
        values = []
        others = []
        for y in range(sy):
            values.append(basis[pl.ds(((sx + 1) * width * 3 + d) * span + y, width, stride=step), :])
            others.append(applied[pl.ds((sx * width * 3 + d) * span + y, width, stride=step), :])
        return carry + product(others, values)

    gram_stiff = lax.fori_loop(0, 3, gram_end, both[:, 0:width])
    values = []
    others = []
    for layer in range(sx + 1):
        for d in range(3):
            values.append(basis[pl.ds(base(layer, 0, d) + sy, width, stride=step), :])
            others.append(applied[pl.ds(out_base(layer, 0, d) + sy, width, stride=step), :])
    gram_stiff = gram_stiff + product(others, values)
    gram_out[...] = jnp.zeros(gram_out.shape, f32)
    gram_out[:, 0:width] = gram_stiff
    gram_out[:, 64 : 64 + width] = both[:, width : 2 * width]


def finish_kernel(sizes, dof, gram, a_in, b_in, stiff_in, mass_in, stiff_gram, mass_gram, search, terms):
    cols, sx, sy, sz = sizes
    eye = (
        lax.broadcasted_iota(jnp.int32, (cols, cols), 0) == lax.broadcasted_iota(jnp.int32, (cols, cols), 1)
    ).astype(f32)
    top = gram[0:cols, 0:cols] * eye
    bottom = gram[0:cols, 64 : 64 + cols] * eye
    quotient = jnp.sum(top, 1, keepdims=True) / jnp.sum(bottom, 1, keepdims=True)
    quotient_row = jnp.sum(top, 0, keepdims=True) / jnp.sum(bottom, 0, keepdims=True)
    for at, out in ((0, stiff_gram), (64, mass_gram)):
        whole = gram[:, at : at + 4 * cols]
        rows = jnp.concatenate(
            [whole[0:cols], whole[cols : 2 * cols] - quotient * whole[2 * cols : 3 * cols], whole[3 * cols :]], 0
        )
        out[:, 0, :] = (1.0 / dof) * jnp.concatenate(
            [
                rows[:, 0:cols],
                rows[:, cols : 2 * cols] - quotient_row * rows[:, 2 * cols : 3 * cols],
                rows[:, 3 * cols :],
            ],
            1,
        )
    squared = quotient * quotient
    powered = 1.0 / (squared * squared)
    coefficient = powered / (jnp.sum(bottom, 1, keepdims=True) * (1.0 / dof))
    weighted = coefficient * quotient
    plane = sx * sy
    total = 0.0
    for j in range(cols):
        here = pl.ds(j * 3 * plane, 3 * plane)
        value = a_in[here, :] - quotient[j : j + 1] * b_in[here, :]
        search[0, j] = value.reshape(3, sx, sy, sz)
        part = pl.ds(j * plane, plane)
        total = total + coefficient[j : j + 1] * stiff_in[part, :] - weighted[j : j + 1] * mass_in[part, :]
    terms[0:plane] = total
    terms[plane : plane + 8] = jnp.broadcast_to(jnp.sum(powered, 0, keepdims=True), (8, sz))


def line(axis, step):
    count = lax.axis_size(axis)
    return [(i, i + step) for i in range(count) if 0 <= i + step < count]


def pairs(axis, first):
    count = lax.axis_size(axis)
    steps = []
    for i in range(first, count - 1, 2):
        steps += [(i, i + 1), (i + 1, i)]
    return steps


def sum_over(value, axis):
    count = lax.axis_size(axis)
    if count & (count - 1):
        return lax.psum(value, axis)
    distance = 1
    while distance < count:
        value = value + lax.ppermute(value, axis, [(i, i ^ distance) for i in range(count)])
        distance *= 2
    return value


def near(value):
    return pltpu.with_memory_space_constraint(value, pltpu.VMEM)


def shards(current, previous, element_stiffness, preconditioner, modulus, density, solid, clamped):
    cols = current.shape[1]
    sx, sy, sz = modulus.shape
    sizes = (cols, sx, sy, sz)
    slabs = cols * 3
    n = slabs * sx
    block = n * sy
    dof = 3.0 * sx * sy * sz * lax.axis_size("bx") * lax.axis_size("by")

    def struct(*shape):
        return jax.ShapeDtypeStruct(shape, f32)

    def kept(*shape, dtype=f32):
        return pltpu.VMEM(shape, dtype)

    own_rows = block + slabs * sy + 5 * sx * sy
    up_rows = -(-(n + 2 * sx) // 8) * 8
    down_rows = -(-(3 * n + 5 * sx) // 8) * 8
    sources = (current, previous, modulus, density, solid, preconditioner, clamped)
    own, prev_free, up, down = pl.pallas_call(
        lambda *refs: prepare_kernel(sizes, *refs),
        in_specs=[pl.BlockSpec(memory_space=pltpu.HBM)] * len(sources),
        scratch_shapes=[pltpu.VMEM(x.shape, x.dtype) for x in sources] + [pltpu.SemaphoreType.DMA((len(sources),))],
        out_shape=(kept(own_rows, sz), kept(block, sz), kept(up_rows, sz), kept(down_rows, sz)),
        compiler_params=pltpu.CompilerParams(vmem_limit_bytes=12 << 20),
        name="prepare",
    )(*[pltpu.with_memory_space_constraint(x, pltpu.HBM) for x in sources])
    from_low = lax.ppermute(up, "by", line("by", 1))
    from_high = lax.ppermute(down, "by", line("by", -1))
    row_pick, col_pick, op_mask = operator_tables(sy)
    op_high, op_low = pl.pallas_call(
        operator_kernel,
        out_shape=(kept(NODE_ROWS + FORCE_ROWS, FORCE_ROWS + EDGE, dtype=bf16),) * 2,
        compiler_params=pltpu.CompilerParams(vmem_limit_bytes=8 << 20),
        name="operator",
    )(element_stiffness, jnp.asarray(row_pick, bf16), jnp.asarray(col_pick, bf16), jnp.asarray(op_mask, bf16))
    pair_a = lax.ppermute(own, "bx", pairs("bx", 0))
    pair_b = lax.ppermute(own, "bx", pairs("bx", 1))
    corner = jnp.concatenate([from_low, from_high], 0)
    corner_a = lax.ppermute(corner, "bx", pairs("bx", 0))
    corner_b = lax.ppermute(corner, "bx", pairs("bx", 1))
    odd = (lax.axis_index("bx") % 2).astype(jnp.int32).reshape(1)
    width = 4 * cols
    vmem = pl.BlockSpec(memory_space=pltpu.VMEM)
    gram, a_part, b_part, stiff_part, mass_part = pl.pallas_call(
        lambda *refs: main_kernel(sizes, *refs),
        in_specs=[pl.BlockSpec(memory_space=pltpu.SMEM)] + [vmem] * 10,
        out_shape=(
            kept(width, 128),
            kept(block, sz),
            kept(block, sz),
            kept(cols * sx * sy, sz),
            kept(cols * sx * sy, sz),
        ),
        scratch_shapes=[
            pltpu.VMEM(((sx + 3) * width * 3 * (sy + 1), sz), f32),
            pltpu.VMEM(((sx + 3) * cols * SLAB, sz), f32),
            pltpu.VMEM(((sx + 1) * width * 3 * (sy + 1), sz), f32),
            pltpu.VMEM(((sx + 2) * sy, sz), f32),
            pltpu.VMEM(((sx + 2) * SLAB, sz), f32),
            pltpu.VMEM(((sx + 2) * SLAB, sz), f32),
            pltpu.VMEM(((sx + 1) * SLAB, sz), f32),
            pltpu.VMEM(((sx + 1) * 3 * SLAB, sz), f32),
        ],
        compiler_params=pltpu.CompilerParams(vmem_limit_bytes=24 << 20),
        name="main",
    )(odd, *[near(x) for x in (own, prev_free, from_low, from_high, pair_a, pair_b, corner_a, corner_b, op_high, op_low)])
    gram = sum_over(sum_over(gram, "bx"), "by")
    stiff_gram, mass_gram, search, terms = pl.pallas_call(
        lambda *refs: finish_kernel(sizes, dof, *refs),
        out_shape=(
            struct(3 * cols, 1, 3 * cols),
            struct(3 * cols, 1, 3 * cols),
            struct(1, cols, 3, sx, sy, sz),
            kept(sx * sy + 8, sz),
        ),
        compiler_params=pltpu.CompilerParams(vmem_limit_bytes=12 << 20),
        name="finish",
    )(*[near(x) for x in (gram, a_part, b_part, stiff_part, mass_part)])
    terms = sum_over(terms, "real")
    share = sz // lax.axis_size("real")
    plane = sx * sy
    mine = lax.dynamic_slice_in_dim(terms[:plane], lax.axis_index("real") * share, share, 1)
    sensitivity = (mine / terms[plane:, :1][:1]).reshape(sx, sy, share)
    return jnp.swapaxes(stiff_gram, 0, 1), jnp.swapaxes(mass_gram, 0, 1), search, sensitivity


def solution(mesh):
    in_specs = (
        P("real", None, None, "bx", "by", None),
        P("real", None, None, "bx", "by", None),
        P(),
        P("real", None, "bx", "by", None),
        P("bx", "by", None),
        P("bx", "by", None),
        P("real", "bx", "by", None),
        P("bx", "by"),
    )
    out_specs = (
        P("real", None, None),
        P("real", None, None),
        P("real", None, None, "bx", "by", None),
        P("bx", "by", "real"),
    )
    return jax.shard_map(shards, mesh=mesh, in_specs=in_specs, out_specs=out_specs, check_vma=False)
```

```python
import numpy as np
import jax
import jax.numpy as jnp
from jax import lax
from jax.experimental import pallas as pl
from jax.experimental.pallas import tpu as pltpu
from jax.sharding import PartitionSpec as P

f32 = jnp.float32
bf16 = jnp.bfloat16
SLAB = 16
NODE_ROWS = 112
FORCE_ROWS = 192
OTHER_TOP = 120
EDGE = 64


def operator_tables(rows):
    row_pick = np.zeros((2, NODE_ROWS + FORCE_ROWS, 24), np.float32)
    col_pick = np.zeros((24, FORCE_ROWS + EDGE), np.float32)
    col_y = np.full(FORCE_ROWS + EDGE, -99)
    for beta in range(24):
        for y in range(rows):
            col_pick[beta, beta * rows + y] = 1
            col_y[beta * rows + y] = y
    for a in range(2):
        for q in range(2):
            for d in range(3):
                for j in range(4):
                    k = FORCE_ROWS + (a * 2 + q) * 16 + d * 4 + j
                    col_pick[(4 * a + 2 * (j % 2) + q) * 3 + d, k] = 1
                    col_y[k] = -1 if j < 2 else rows
    mask = np.zeros((2, NODE_ROWS + FORCE_ROWS, FORCE_ROWS + EDGE), np.float32)
    for q in range(2):
        for a in range(2):
            for d in range(3):
                for y in range(rows + 1):
                    m = (q * 6 + a * 3 + d) * rows + y
                    if y == rows:
                        m = 12 * rows + q * 8 + a * 3 + d
                    for b in range(2):
                        row_pick[b, m, (4 * a + 2 * b + q) * 3 + d] = 1
                        mask[b, m] = col_y == y - b
    for alpha in range(24):
        for y in range(rows):
            m = NODE_ROWS + alpha * rows + y
            row_pick[0, m, alpha] = 1
            mask[0, m, :FORCE_ROWS] = col_y[:FORCE_ROWS] == y
    return row_pick, col_pick, mask


def split(value):
    high = value.astype(bf16)
    return high, (value - high.astype(f32)).astype(bf16)


def dot(left, right):
    return jnp.dot(left, right, preferred_element_type=f32)


def fetch(sources, buffers, arrived):
    copies = [pltpu.make_async_copy(source, buffer, arrived.at[i]) for i, (source, buffer) in enumerate(zip(sources, buffers))]
    for copy in copies:
        copy.start()
    for copy in copies:
        copy.wait()
    return buffers


def operator_kernel(*refs):
    high_out, low_out = refs[4:6]
    matrix, row_pick, col_pick, mask = fetch(refs[0:4], refs[6:10], refs[10])
    high, low = split(matrix[...])
    for part, out in ((high, high_out), (low, low_out)):
        total = 0.0
        for b in range(2):
            picked = dot(row_pick[b], part).astype(bf16)
            total = total + dot(picked, col_pick[...]) * mask[b].astype(f32)
        out[...] = total.astype(bf16)


def prepare_kernel(sizes, *refs):
    own, prev_free, up, down = refs[7:11]
    cur, prev, modulus, density, solid, precond, clamped = fetch(refs[0:7], refs[11:18], refs[18])
    cols, sx, sy, sz = sizes
    slabs = cols * 3
    block = slabs * sx * sy
    held = clamped[...].astype(f32)
    eye = (lax.broadcasted_iota(jnp.int32, (sy, sy), 0) == lax.broadcasted_iota(jnp.int32, (sy, sy), 1)).astype(f32)
    bottom = (lax.broadcasted_iota(jnp.int32, (sy, sz), 1) == 0).astype(f32)
    planes = []
    for x in range(sx):
        column = jnp.sum(jnp.broadcast_to(held[x : x + 1], (sy, sy)) * eye, 1, keepdims=True)
        planes.append((1.0 - column * bottom)[None])
    free = jnp.concatenate(planes, 0)
    share = solid[0].astype(f32)
    own[0:block] = (cur[0] * free[None, None]).reshape(block, sz)
    masked = prev[0] * free[None, None]
    prev_free[...] = masked.reshape(block, sz)
    own[block : block + slabs * sy] = masked[:, :, 0].reshape(slabs * sy, sz)
    field = block + slabs * sy
    plane = sx * sy
    own[field : field + plane] = (modulus[...] * (0.02 + 0.98 * share)).reshape(plane, sz)
    own[field + plane : field + 2 * plane] = (density[...] * (0.1 + 0.9 * share) * 0.125).reshape(plane, sz)
    own[field + 2 * plane : field + 5 * plane] = (precond[0] * free[None]).reshape(3 * plane, sz)
    n = slabs * sx
    up[0:n] = own[pl.ds(sy - 1, n, stride=sy), :]
    up[n : n + 2 * sx] = own[pl.ds(field + sy - 1, 2 * sx, stride=sy), :]
    up[n + 2 * sx :] = jnp.zeros((up.shape[0] - n - 2 * sx, sz), f32)
    down[0:n] = own[pl.ds(0, n, stride=sy), :]
    down[n : 2 * n] = own[pl.ds(1, n, stride=sy), :]
    down[2 * n : 3 * n] = prev_free[pl.ds(0, n, stride=sy), :]
    down[3 * n : 3 * n + 5 * sx] = own[pl.ds(field, 5 * sx, stride=sy), :]
    down[3 * n + 5 * sx :] = jnp.zeros((down.shape[0] - 3 * n - 5 * sx, sz), f32)


def helpers(sizes, basis, stiff, op_high, op_low):
    cols, _, sy, sz = sizes
    width = 4 * cols
    span = sy + 1
    lane = lax.broadcasted_iota(jnp.int32, (8, sz), 1)
    not_last = (lane < sz - 1).astype(f32)
    not_first = (lane > 0).astype(f32)

    def base(layer, k, d):
        return (((layer + 1) * width + k) * 3 + d) * span

    def out_base(layer, k, d):
        return ((layer * width + k) * 3 + d) * span

    def corner_tiles(k, layer):
        tiles = []
        for a in range(2):
            for b in range(2):
                near = [basis[pl.ds(base(layer + a, k, d) + b, sy), :] for d in range(3)]
                tiles += near
                tiles += [pltpu.roll(tile, sz - 1, 1) for tile in near]
        return tiles

    def weights(layer):
        plain = stiff[pl.ds((layer + 1) * sy, sy), :]
        return plain, plain * not_last

    def scaled(tiles, layer):
        plain, cut = weights(layer)
        return [tile * (cut if (i // 3) % 2 else plain) for i, tile in enumerate(tiles)]

    def apply(columns, rows, depth):
        value = jnp.concatenate(columns, 1)
        high = value.astype(bf16)
        rest = value - high.astype(f32)
        both = dot(jnp.concatenate([op_high[0:rows, 0:depth], op_low[0:rows, 0:depth]], 0), high)
        total = both[0:rows] + both[rows:]
        nodes = total[0:NODE_ROWS] + dot(op_high[0:NODE_ROWS, 0:depth], rest.astype(bf16))
        return nodes, total[NODE_ROWS:], value[0:FORCE_ROWS] + rest[0:FORCE_ROWS]

    def node_parts(out):
        parts = []
        for i in range(6):
            shifted = pltpu.roll(out[(6 + i) * sy : (7 + i) * sy], 1, 1) * not_first
            parts.append(out[i * sy : (i + 1) * sy] + shifted)
        rim = out[12 * sy : 12 * sy + 8] + pltpu.roll(out[12 * sy + 8 : 12 * sy + 16], 1, 1) * not_first
        return parts, rim

    return base, out_base, not_last, not_first, corner_tiles, weights, scaled, apply, node_parts


def current_kernel(
    sizes, place, own, prev_free, from_low, from_high,
    pair_a, pair_b, corner_a, corner_b, op_high, op_low,
    basis, applied, a_out, b_out, stiff_out, mass_out, share_out, stiff, lumped,
    edge, stiff_edge, mass_rows, scale, above, below,
):
    cols, sx, sy, sz = sizes
    slabs = cols * 3
    block = slabs * sx * sy
    plane = sx * sy
    field = block + slabs * sy
    low_rows = from_low.shape[0]
    n = slabs * sx
    span = sy + 1

    base, out_base, not_last, not_first, corner_tiles, weights, scaled, apply, node_parts = helpers(
        sizes, basis, stiff, op_high, op_low
    )

    def unpack(layer, source, low, high, at):
        low_ref, low_at = low
        high_ref, high_at = high
        for k in range(cols):
            for d in range(3):
                basis[pl.ds(base(layer, k, d), sy), :] = source[pl.ds(((k * 3 + d) * sx + at) * sy, sy), :]
        basis[pl.ds(base(layer, 0, 0) + sy, slabs, stride=span), :] = high_ref[pl.ds(high_at + at, slabs, stride=sx), :]
        for d in range(3):
            start = (layer + 1) * cols * SLAB + d * 4
            pick = d * sx + at
            edge[pl.ds(start, cols, stride=SLAB), :] = low_ref[pl.ds(low_at + pick, cols, stride=3 * sx), :]
            edge[pl.ds(start + 1, cols, stride=SLAB), :] = source[pl.ds(pick * sy, cols, stride=3 * sx * sy), :]
            edge[pl.ds(start + 2, cols, stride=SLAB), :] = high_ref[pl.ds(high_at + pick, cols, stride=3 * sx), :]
            edge[pl.ds(start + 3, cols, stride=SLAB), :] = high_ref[pl.ds(high_at + n + pick, cols, stride=3 * sx), :]

    def unpack_fields(layer, source, low, high, at):
        low_ref, low_at = low
        high_ref, high_at = high
        index = layer + 1
        stiff[pl.ds(index * sy, sy), :] = source[pl.ds(field + at * sy, sy), :]
        before = low_ref[pl.ds(low_at + n + at, 1), :]
        after = high_ref[pl.ds(high_at + 3 * n + at, 1), :]
        for j in range(4):
            row = before if j < 2 else after
            stiff_edge[pl.ds(index * SLAB + j, 3, stride=4), :] = jnp.broadcast_to(row, (3, sz))
        mass_rows[pl.ds(index * SLAB, 1), :] = low_ref[pl.ds(low_at + n + sx + at, 1), :]
        mass_rows[pl.ds(index * SLAB + 1, sy), :] = source[pl.ds(field + plane + at * sy, sy), :]
        mass_rows[pl.ds(index * SLAB + 1 + sy, 1), :] = high_ref[pl.ds(high_at + 3 * n + sx + at, 1), :]

    def unpack_nodes(layer, source, prev_source, high, at, prev_stride, prev_at):
        high_ref, high_at = high
        for k in range(cols):
            for d in range(3):
                basis[pl.ds(base(layer, 3 * cols + k, d), sy), :] = prev_source[
                    pl.ds(prev_at + ((k * 3 + d) * prev_stride) * sy, sy), :
                ]
        basis[pl.ds(base(layer, 3 * cols, 0) + sy, slabs, stride=span), :] = high_ref[
            pl.ds(high_at + 2 * n + at, slabs, stride=sx), :
        ]
        for d in range(3):
            scale[pl.ds((layer * 3 + d) * SLAB, sy), :] = source[pl.ds(field + 2 * plane + (d * sx + at) * sy, sy), :]
        scale[pl.ds(layer * 3 * SLAB + sy, 3, stride=SLAB), :] = high_ref[pl.ds(high_at + 3 * n + 2 * sx + at, 3, stride=sx), :]

    edge[...] = jnp.zeros(edge.shape, f32)
    stiff_edge[...] = jnp.zeros(stiff_edge.shape, f32)
    own_low = (from_low, 0)
    own_high = (from_high, 0)
    for layer in range(sx):
        unpack(layer, own, own_low, own_high, layer)
        unpack_fields(layer, own, own_low, own_high, layer)
        unpack_nodes(layer, own, prev_free, own_high, layer, sx, layer * sy)

    def unpack_sides(lower, lower_corner, upper, upper_corner):
        lower_high = (lower_corner, low_rows)
        unpack(-1, lower, (lower_corner, 0), lower_high, sx - 1)
        unpack_fields(-1, lower, (lower_corner, 0), lower_high, sx - 1)
        upper_high = (upper_corner, low_rows)
        for step in range(2):
            unpack(sx + step, upper, (upper_corner, 0), upper_high, step)
        unpack_fields(sx, upper, (upper_corner, 0), upper_high, 0)
        unpack_nodes(sx, upper, upper, upper_high, 0, 1, block)

    @pl.when(place[0] == 1)
    def _():
        unpack_sides(pair_a, corner_a, pair_b, corner_b)

    @pl.when(place[0] == 0)
    def _():
        unpack_sides(pair_b, corner_b, pair_a, corner_a)

    for layer in range(sx + 1):
        first = layer * SLAB
        second = first + SLAB
        mass_sum = mass_rows[pl.ds(first, SLAB), :] + mass_rows[pl.ds(second, SLAB), :]
        lumped[pl.ds(layer * SLAB, SLAB), :] = mass_sum
        inner = lumped[pl.ds(layer * SLAB, sy), :] + lumped[pl.ds(layer * SLAB + 1, sy), :]
        outer = lumped[pl.ds(layer * SLAB + sy, 1), :] + lumped[pl.ds(layer * SLAB + sy + 1, 1), :]
        lumped[pl.ds(layer * SLAB, sy), :] = inner + pltpu.roll(inner, 1, 1) * not_first
        outer = jnp.broadcast_to(outer, (8, sz))
        outer = outer + pltpu.roll(outer, 1, 1) * not_first
        lumped[pl.ds(layer * SLAB + sy, 1), :] = outer[0:1]

    def edge_tiles(k, layer):
        plain = stiff_edge[pl.ds((layer + 1) * SLAB, SLAB), :]
        cut = plain * jnp.concatenate([not_last, not_last], 0)
        tiles = []
        for a in range(2):
            tile = edge[pl.ds(((layer + 1 + a) * cols + k) * SLAB, SLAB), :]
            tiles.append(tile * plain)
            tiles.append(pltpu.roll(tile, sz - 1, 1) * cut)
        return tiles

    above[...] = jnp.zeros(above.shape, f32)
    below[...] = jnp.zeros(below.shape, f32)

    def current_pair(pair, carry):
        sums = [[0.0, 0.0], [0.0, 0.0]]
        tails = [None, None]
        for layer in range(-1, sx + 1):
            inner = 0 <= layer < sx
            columns = []
            kept = []
            for c in range(2):
                k = pair * 2 + c
                tiles = corner_tiles(k, layer)
                kept.append(tiles)
                columns.append(jnp.concatenate(scaled(tiles, layer) + edge_tiles(k, layer), 0))
            out, forces, doubled = apply(columns, NODE_ROWS + FORCE_ROWS if inner else NODE_ROWS, FORCE_ROWS + EDGE)
            for c in range(2):
                k = pair * 2 + c
                part = out[:, c * sz : (c + 1) * sz]
                if inner:
                    work = forces[:, c * sz : (c + 1) * sz] * doubled[:, c * sz : (c + 1) * sz]
                    energy = 0.0
                    square = [0.0, 0.0]
                    for alpha in range(24):
                        q = (alpha // 3) % 2
                        tile = kept[c][alpha]
                        energy = energy + work[alpha * sy : (alpha + 1) * sy]
                        square[q] = square[q] + tile * tile
                    at = (k * sx + layer) * sy
                    mass = mass_rows[pl.ds((layer + 1) * SLAB + 1, sy), :]
                    stiff_out[pl.ds(at, sy), :] = energy * (3.0 / weights(layer)[0])
                    mass_out[pl.ds(at, sy), :] = mass * (square[0] + square[1] * not_last)
                parts, rim = node_parts(part)
                if layer >= 0:
                    before, rim_before = tails[c]
                    rim_sum = rim[0:3] + rim_before[3:6]
                    load = lumped[pl.ds(layer * SLAB, SLAB), :]
                    for d in range(3):
                        total = parts[d] + before[3 + d]
                        factor = scale[pl.ds((layer * 3 + d) * SLAB, SLAB), :]
                        a_value = factor[0:sy] * total
                        both = factor * load
                        b_value = both[0:sy] * basis[pl.ds(base(layer, k, d), sy), :]
                        b_rim = both[sy : sy + 1] * basis[pl.ds(base(layer, k, d) + sy, 1), :]
                        basis[pl.ds(base(layer, cols + k, d), sy), :] = a_value
                        basis[pl.ds(base(layer, cols + k, d) + sy, 1), :] = factor[sy : sy + 1] * rim_sum[d : d + 1]
                        basis[pl.ds(base(layer, 2 * cols + k, d), sy), :] = b_value
                        basis[pl.ds(base(layer, 2 * cols + k, d) + sy, 1), :] = b_rim
                        if layer < sx:
                            value = basis[pl.ds(base(layer, k, d), sy), :]
                            sums[c][0] = sums[c][0] + value * total
                            sums[c][1] = sums[c][1] + value * value * load[0:sy]
                            applied[pl.ds(out_base(layer, k, d), sy), :] = total
                            at = ((k * 3 + d) * sx + layer) * sy
                            a_out[pl.ds(at, sy), :] = a_value
                            b_out[pl.ds(at, sy), :] = b_value
                        else:
                            applied[pl.ds(out_base(layer, k, d), sy), :] = jnp.zeros((sy, sz), f32)
                        applied[pl.ds(out_base(layer, k, d) + sy, 1), :] = jnp.zeros((1, sz), f32)
                tails[c] = (parts, rim)
        for c in range(2):
            above[pl.ds(pair * 2 + c, 1), :] = jnp.sum(sums[c][0], 0, keepdims=True)
            below[pl.ds(pair * 2 + c, 1), :] = jnp.sum(sums[c][1], 0, keepdims=True)
        return carry

    lax.fori_loop(0, cols // 2, current_pair, 0, unroll=cols // 2)

    half = sz // 2
    rows = cols * sx * sy
    wide = lax.broadcasted_iota(jnp.int32, (rows, sz), 1)
    stiff_all = stiff_out[...]
    mass_all = mass_out[...]
    first = place[1] == 0
    stiff_half = jnp.where(first, pltpu.roll(stiff_all, half, 1), stiff_all)
    mass_half = jnp.where(first, mass_all, pltpu.roll(mass_all, half, 1))
    share_out[0:rows] = jnp.where(wide < half, stiff_half, mass_half)
    spot = lax.broadcasted_iota(jnp.int32, above.shape, 1)
    top = jnp.sum(above[...], 1, keepdims=True)
    bottom = jnp.sum(below[...], 1, keepdims=True)
    share_out[rows:] = jnp.where(spot == OTHER_TOP, top, 0.0) + jnp.where(spot == OTHER_TOP + 1, bottom, 0.0)


def gram_kernel(sizes, basis, stiff, lumped, op_high, op_low, applied_in, applied, gram_out):
    cols, sx, sy, sz = sizes
    width = 4 * cols
    span = sy + 1
    base, out_base, _, _, corner_tiles, _, scaled, apply, node_parts = helpers(sizes, basis, stiff, op_high, op_low)

    def other_pair(pair, carry):
        tails = [None, None]
        for layer in range(sx):
            columns = []
            for c in range(2):
                k = cols + pair * 2 + c
                columns.append(jnp.concatenate(scaled(corner_tiles(k, layer), layer), 0))
            out = apply(columns, NODE_ROWS, FORCE_ROWS)[0]
            for c in range(2):
                k = cols + pair * 2 + c
                parts, rim = node_parts(out[:, c * sz : (c + 1) * sz])
                ends = [(layer, parts[0:3], rim[0:3], tails[c])]
                if layer == sx - 1:
                    ends.append((sx, parts[3:6], rim[3:6], None))
                for at, values, row, before in ends:
                    for d in range(3):
                        value = values[d]
                        last = row[d : d + 1]
                        if before is not None:
                            value = value + before[0][3 + d]
                            last = last + before[1][3 + d : 4 + d]
                        applied[pl.ds(out_base(at, k, d), sy), :] = value
                        applied[pl.ds(out_base(at, k, d) + sy, 1), :] = last
                tails[c] = (parts, rim)
        return carry

    lax.fori_loop(0, 3 * cols // 2, other_pair, 0, unroll=3 * cols // 2)

    def contract(left, right):
        return lax.dot_general(left, right, (((1,), (1,)), ((), ())), preferred_element_type=f32)

    step = 3 * span

    def product(applied_values, basis_values):
        left_high, left_low = split(jnp.concatenate(basis_values, 1))
        right_high, right_low = split(jnp.concatenate(applied_values, 1))
        rows = left_high.shape[0]
        both = contract(jnp.concatenate([left_high, left_low], 0), right_high)
        return both[0:rows] + both[rows:] + contract(left_high, right_low)

    def gram_group(index, carry):
        layer = index // 3
        d = index - layer * 3
        values = []
        others = []
        for y in range(sy):
            value = basis[pl.ds(((layer + 1) * width * 3 + d) * span + y, width, stride=step), :]
            other = applied[pl.ds((layer * width * 3 + d) * span + y, width, stride=step), :]
            values.append(value)
            others.append(jnp.concatenate([other, value * lumped[pl.ds(layer * SLAB + y, 1), :]], 0))
        return carry + product(others, values)

    both = lax.fori_loop(0, 3 * sx, gram_group, jnp.zeros((width, 2 * width), f32))

    def gram_end(d, carry):
        values = []
        others = []
        for y in range(sy):
            values.append(basis[pl.ds(((sx + 1) * width * 3 + d) * span + y, width, stride=step), :])
            others.append(applied[pl.ds((sx * width * 3 + d) * span + y, width, stride=step), :])
        return carry + product(others, values)

    gram_stiff = lax.fori_loop(0, 3, gram_end, both[:, 0:width])
    values = []
    others = []
    for layer in range(sx + 1):
        for d in range(3):
            values.append(basis[pl.ds(base(layer, 0, d) + sy, width, stride=step), :])
            others.append(applied[pl.ds(out_base(layer, 0, d) + sy, width, stride=step), :])
    gram_stiff = gram_stiff + product(others, values)
    gram_out[...] = jnp.zeros(gram_out.shape, f32)
    gram_out[:, 0:width] = gram_stiff
    gram_out[:, 64 : 64 + width] = both[:, width : 2 * width]


def finish_kernel(
    sizes, dof, place, gram, a_in, b_in, stiff_in, mass_in, other, stiff_gram, mass_gram, search, sensitivity
):
    cols, sx, sy, sz = sizes
    eye = (
        lax.broadcasted_iota(jnp.int32, (cols, cols), 0) == lax.broadcasted_iota(jnp.int32, (cols, cols), 1)
    ).astype(f32)
    top = gram[0:cols, 0:cols] * eye
    bottom = gram[0:cols, 64 : 64 + cols] * eye
    quotient = jnp.sum(top, 1, keepdims=True) / jnp.sum(bottom, 1, keepdims=True)
    quotient_row = jnp.sum(top, 0, keepdims=True) / jnp.sum(bottom, 0, keepdims=True)
    for at, out in ((0, stiff_gram), (64, mass_gram)):
        whole = gram[:, at : at + 4 * cols]
        rows = jnp.concatenate(
            [whole[0:cols], whole[cols : 2 * cols] - quotient * whole[2 * cols : 3 * cols], whole[3 * cols :]], 0
        )
        out[:, 0, :] = (1.0 / dof) * jnp.concatenate(
            [
                rows[:, 0:cols],
                rows[:, cols : 2 * cols] - quotient_row * rows[:, 2 * cols : 3 * cols],
                rows[:, 3 * cols :],
            ],
            1,
        )

    def weigh(value, total):
        squared = value * value
        powered = 1.0 / (squared * squared)
        factor = powered / (total * (1.0 / dof))
        return jnp.sum(powered, 0, keepdims=True), factor, factor * value

    overall, coefficient, weighted = weigh(quotient, jnp.sum(bottom, 1, keepdims=True))
    other_total = gram[0:cols, OTHER_TOP + 1 : OTHER_TOP + 2]
    other_sum, other_coefficient, other_weighted = weigh(gram[0:cols, OTHER_TOP : OTHER_TOP + 1] / other_total, other_total)
    half = sz // 2
    spot = lax.broadcasted_iota(jnp.int32, (cols, sz), 1)
    other_factor = jnp.where(spot < half, other_coefficient, -other_weighted)
    plane = sx * sy
    mine = 0.0
    received = 0.0
    for j in range(cols):
        here = pl.ds(j * 3 * plane, 3 * plane)
        value = a_in[here, :] - quotient[j : j + 1] * b_in[here, :]
        search[0, j] = value.reshape(3, sx, sy, sz)
        part = pl.ds(j * plane, plane)
        mine = mine + coefficient[j : j + 1] * stiff_in[part, :] - weighted[j : j + 1] * mass_in[part, :]
        received = received + other_factor[j : j + 1] * other[part, :]
    received = received + pltpu.roll(received, half, 1)
    mine = jnp.where(place[1] == 0, mine, pltpu.roll(mine, half, 1))
    total = (mine + received) / (overall + other_sum)
    sensitivity[...] = total[:, 0:half].reshape(sx, sy, half)


def line(axis, step):
    count = lax.axis_size(axis)
    return [(i, i + step) for i in range(count) if 0 <= i + step < count]


def pairs(axis, first):
    count = lax.axis_size(axis)
    steps = []
    for i in range(first, count - 1, 2):
        steps += [(i, i + 1), (i + 1, i)]
    return steps


def sum_over(value, axis):
    count = lax.axis_size(axis)
    if count & (count - 1):
        return lax.psum(value, axis)
    distance = 1
    while distance < count:
        value = value + lax.ppermute(value, axis, [(i, i ^ distance) for i in range(count)])
        distance *= 2
    return value


def near(value):
    return pltpu.with_memory_space_constraint(value, pltpu.VMEM)


def far(value):
    return pltpu.with_memory_space_constraint(value, pltpu.HBM)


def shards(current, previous, element_stiffness, preconditioner, modulus, density, solid, clamped):
    cols = current.shape[1]
    sx, sy, sz = modulus.shape
    sizes = (cols, sx, sy, sz)
    slabs = cols * 3
    n = slabs * sx
    block = n * sy
    dof = 3.0 * sx * sy * sz * lax.axis_size("bx") * lax.axis_size("by")

    def struct(*shape):
        return jax.ShapeDtypeStruct(shape, f32)

    def kept(*shape, dtype=f32):
        return pltpu.VMEM(shape, dtype)

    own_rows = block + slabs * sy + 5 * sx * sy
    up_rows = -(-(n + 2 * sx) // 8) * 8
    down_rows = -(-(3 * n + 5 * sx) // 8) * 8
    sources = (current, previous, modulus, density, solid, preconditioner, clamped)
    own, prev_free, up, down = pl.pallas_call(
        lambda *refs: prepare_kernel(sizes, *refs),
        in_specs=[pl.BlockSpec(memory_space=pltpu.HBM)] * len(sources),
        scratch_shapes=[pltpu.VMEM(x.shape, x.dtype) for x in sources] + [pltpu.SemaphoreType.DMA((len(sources),))],
        out_shape=(kept(own_rows, sz), kept(block, sz), kept(up_rows, sz), kept(down_rows, sz)),
        compiler_params=pltpu.CompilerParams(vmem_limit_bytes=12 << 20),
        name="prepare",
    )(*[far(x) for x in sources])
    from_low = lax.ppermute(up, "by", line("by", 1))
    from_high = lax.ppermute(down, "by", line("by", -1))
    row_pick, col_pick, op_mask = operator_tables(sy)
    tables = (element_stiffness, jnp.asarray(row_pick, bf16), jnp.asarray(col_pick, bf16), jnp.asarray(op_mask, bf16))
    op_high, op_low = pl.pallas_call(
        operator_kernel,
        in_specs=[pl.BlockSpec(memory_space=pltpu.HBM)] * len(tables),
        out_shape=(kept(NODE_ROWS + FORCE_ROWS, FORCE_ROWS + EDGE, dtype=bf16),) * 2,
        scratch_shapes=[pltpu.VMEM(x.shape, x.dtype) for x in tables] + [pltpu.SemaphoreType.DMA((len(tables),))],
        compiler_params=pltpu.CompilerParams(vmem_limit_bytes=8 << 20),
        name="operator",
    )(*[far(x) for x in tables])
    pair_a = lax.ppermute(own, "bx", pairs("bx", 0))
    pair_b = lax.ppermute(own, "bx", pairs("bx", 1))
    from_low, from_high, op_high, op_low = lax.optimization_barrier((from_low, from_high, op_high, op_low))
    corner = jnp.concatenate([from_low, from_high], 0)
    corner_a = lax.ppermute(corner, "bx", pairs("bx", 0))
    corner_b = lax.ppermute(corner, "bx", pairs("bx", 1))
    place = jnp.stack([lax.axis_index("bx") % 2, lax.axis_index("real")]).astype(jnp.int32)
    width = 4 * cols
    span = sy + 1
    energies = cols * sx * sy
    vmem = pl.BlockSpec(memory_space=pltpu.VMEM)
    smem = pl.BlockSpec(memory_space=pltpu.SMEM)
    basis, applied, a_part, b_part, stiff_part, mass_part, shared, stiff, lumped = pl.pallas_call(
        lambda *refs: current_kernel(sizes, *refs),
        in_specs=[smem] + [vmem] * 10,
        out_shape=(
            kept((sx + 3) * width * 3 * span, sz),
            kept((sx + 1) * width * 3 * span, sz),
            kept(block, sz),
            kept(block, sz),
            kept(energies, sz),
            kept(energies, sz),
            kept(energies + 16, sz),
            kept((sx + 2) * sy, sz),
            kept((sx + 1) * SLAB, sz),
        ),
        scratch_shapes=[
            pltpu.VMEM(((sx + 3) * cols * SLAB, sz), f32),
            pltpu.VMEM(((sx + 2) * SLAB, sz), f32),
            pltpu.VMEM(((sx + 2) * SLAB, sz), f32),
            pltpu.VMEM(((sx + 1) * 3 * SLAB, sz), f32),
            pltpu.VMEM((16, sz), f32),
            pltpu.VMEM((16, sz), f32),
        ],
        compiler_params=pltpu.CompilerParams(vmem_limit_bytes=16 << 20),
        name="current",
    )(place, *[near(x) for x in (own, prev_free, from_low, from_high, pair_a, pair_b, corner_a, corner_b, op_high, op_low)])
    count = lax.axis_size("real")
    other = lax.ppermute(shared, "real", [(i, (i + 1) % count) for i in range(count)])
    _, gram = pl.pallas_call(
        lambda *refs: gram_kernel(sizes, *refs),
        in_specs=[vmem] * 6,
        out_shape=(kept((sx + 1) * width * 3 * span, sz), kept(width, 128)),
        input_output_aliases={5: 0},
        compiler_params=pltpu.CompilerParams(vmem_limit_bytes=16 << 20),
        name="gram",
    )(*[near(x) for x in (basis, stiff, lumped, op_high, op_low, applied)])
    gram = jnp.concatenate([gram[0:16] + other[energies:], gram[16:]], 0)
    gram = sum_over(sum_over(gram, "bx"), "by")
    stiff_gram, mass_gram, search, sensitivity = pl.pallas_call(
        lambda *refs: finish_kernel(sizes, dof, *refs),
        in_specs=[smem] + [vmem] * 6,
        out_shape=(
            struct(3 * cols, 1, 3 * cols),
            struct(3 * cols, 1, 3 * cols),
            struct(1, cols, 3, sx, sy, sz),
            struct(sx, sy, sz // 2),
        ),
        compiler_params=pltpu.CompilerParams(vmem_limit_bytes=12 << 20),
        name="finish",
    )(place, *[near(x) for x in (gram, a_part, b_part, stiff_part, mass_part, other)])
    return jnp.swapaxes(stiff_gram, 0, 1), jnp.swapaxes(mass_gram, 0, 1), search, sensitivity


def solution(mesh):
    in_specs = (
        P("real", None, None, "bx", "by", None),
        P("real", None, None, "bx", "by", None),
        P(),
        P("real", None, "bx", "by", None),
        P("bx", "by", None),
        P("bx", "by", None),
        P("real", "bx", "by", None),
        P("bx", "by"),
    )
    out_specs = (
        P("real", None, None),
        P("real", None, None),
        P("real", None, None, "bx", "by", None),
        P("bx", "by", "real"),
    )
    return jax.shard_map(shards, mesh=mesh, in_specs=in_specs, out_specs=out_specs, check_vma=False)
```

```python
import numpy as np
import jax
import jax.numpy as jnp
from jax import lax
from jax.experimental import pallas as pl
from jax.experimental.pallas import tpu as pltpu
from jax.sharding import PartitionSpec as P

f32 = jnp.float32
bf16 = jnp.bfloat16
SLAB = 16
NODE_ROWS = 112
FORCE_ROWS = 192
OTHER_TOP = 120
EDGE = 64


def operator_tables(rows):
    row_pick = np.zeros((2, NODE_ROWS + FORCE_ROWS, 24), np.float32)
    col_pick = np.zeros((24, FORCE_ROWS + EDGE), np.float32)
    col_y = np.full(FORCE_ROWS + EDGE, -99)
    for beta in range(24):
        for y in range(rows):
            col_pick[beta, beta * rows + y] = 1
            col_y[beta * rows + y] = y
    for a in range(2):
        for q in range(2):
            for d in range(3):
                for j in range(4):
                    k = FORCE_ROWS + (a * 2 + q) * 16 + d * 4 + j
                    col_pick[(4 * a + 2 * (j % 2) + q) * 3 + d, k] = 1
                    col_y[k] = -1 if j < 2 else rows
    mask = np.zeros((2, NODE_ROWS + FORCE_ROWS, FORCE_ROWS + EDGE), np.float32)
    for q in range(2):
        for a in range(2):
            for d in range(3):
                for y in range(rows + 1):
                    m = (q * 6 + a * 3 + d) * rows + y
                    if y == rows:
                        m = 12 * rows + q * 8 + a * 3 + d
                    for b in range(2):
                        row_pick[b, m, (4 * a + 2 * b + q) * 3 + d] = 1
                        mask[b, m] = col_y == y - b
    for alpha in range(24):
        for y in range(rows):
            m = NODE_ROWS + alpha * rows + y
            row_pick[0, m, alpha] = 1
            mask[0, m, :FORCE_ROWS] = col_y[:FORCE_ROWS] == y
    return row_pick, col_pick, mask


def split(value):
    high = value.astype(bf16)
    return high, (value - high.astype(f32)).astype(bf16)


def dot(left, right):
    return jnp.dot(left, right, preferred_element_type=f32)


def fetch(sources, buffers, arrived):
    copies = [pltpu.make_async_copy(source, buffer, arrived.at[i]) for i, (source, buffer) in enumerate(zip(sources, buffers))]
    for copy in copies:
        copy.start()
    for copy in copies:
        copy.wait()
    return buffers


def operator_kernel(*refs):
    high_out, low_out = refs[4:6]
    matrix, row_pick, col_pick, mask = fetch(refs[0:4], refs[6:10], refs[10])
    high, low = split(matrix[...])
    for part, out in ((high, high_out), (low, low_out)):
        total = 0.0
        for b in range(2):
            picked = dot(row_pick[b], part).astype(bf16)
            total = total + dot(picked, col_pick[...]) * mask[b].astype(f32)
        out[...] = total.astype(bf16)


def prepare_kernel(sizes, odd, *refs):
    own, prev_free, message_a, message_b = refs[7:11]
    cur, prev, modulus, density, solid, precond, clamped = fetch(refs[0:7], refs[11:18], refs[18])
    cols, sx, sy, sz = sizes
    slabs = cols * 3
    block = slabs * sx * sy
    held = clamped[...].astype(f32)
    eye = (lax.broadcasted_iota(jnp.int32, (sy, sy), 0) == lax.broadcasted_iota(jnp.int32, (sy, sy), 1)).astype(f32)
    bottom = (lax.broadcasted_iota(jnp.int32, (sy, sz), 1) == 0).astype(f32)
    planes = []
    for x in range(sx):
        column = jnp.sum(jnp.broadcast_to(held[x : x + 1], (sy, sy)) * eye, 1, keepdims=True)
        planes.append((1.0 - column * bottom)[None])
    free = jnp.concatenate(planes, 0)
    share = solid[0].astype(f32)
    own[0:block] = (cur[0] * free[None, None]).reshape(block, sz)
    masked = prev[0] * free[None, None]
    prev_free[...] = masked.reshape(block, sz)
    own[block : block + slabs * sy] = masked[:, :, 0].reshape(slabs * sy, sz)
    field = block + slabs * sy
    plane = sx * sy
    own[field : field + plane] = (modulus[...] * (0.02 + 0.98 * share)).reshape(plane, sz)
    own[field + plane : field + 2 * plane] = (density[...] * (0.1 + 0.9 * share) * 0.125).reshape(plane, sz)
    own[field + 2 * plane : field + 5 * plane] = (precond[0] * free[None]).reshape(3 * plane, sz)
    n = slabs * sx

    def fill(up, down):
        up[0:n] = own[pl.ds(sy - 1, n, stride=sy), :]
        up[n : n + 2 * sx] = own[pl.ds(field + sy - 1, 2 * sx, stride=sy), :]
        down[0:n] = own[pl.ds(0, n, stride=sy), :]
        down[n : 2 * n] = own[pl.ds(1, n, stride=sy), :]
        down[2 * n : 3 * n] = prev_free[pl.ds(0, n, stride=sy), :]
        down[3 * n : 3 * n + 5 * sx] = own[pl.ds(field, 5 * sx, stride=sy), :]

    @pl.when(odd[0] == 1)
    def _():
        fill(message_b, message_a)

    @pl.when(odd[0] == 0)
    def _():
        fill(message_a, message_b)


def helpers(sizes, basis, stiff, op_high, op_low):
    cols, _, sy, sz = sizes
    width = 4 * cols
    span = sy + 1
    lane = lax.broadcasted_iota(jnp.int32, (8, sz), 1)
    not_last = (lane < sz - 1).astype(f32)
    not_first = (lane > 0).astype(f32)

    def base(layer, k, d):
        return (((layer + 1) * width + k) * 3 + d) * span

    def out_base(layer, k, d):
        return ((layer * width + k) * 3 + d) * span

    def corner_tiles(k, layer):
        tiles = []
        for a in range(2):
            for b in range(2):
                near = [basis[pl.ds(base(layer + a, k, d) + b, sy), :] for d in range(3)]
                tiles += near
                tiles += [pltpu.roll(tile, sz - 1, 1) for tile in near]
        return tiles

    def weights(layer):
        plain = stiff[pl.ds((layer + 1) * sy, sy), :]
        return plain, plain * not_last

    def scaled(tiles, layer):
        plain, cut = weights(layer)
        return [tile * (cut if (i // 3) % 2 else plain) for i, tile in enumerate(tiles)]

    def apply(columns, rows, depth):
        value = jnp.concatenate(columns, 1)
        high = value.astype(bf16)
        rest = value - high.astype(f32)
        both = dot(jnp.concatenate([op_high[0:rows, 0:depth], op_low[0:rows, 0:depth]], 0), high)
        total = both[0:rows] + both[rows:]
        nodes = total[0:NODE_ROWS] + dot(op_high[0:NODE_ROWS, 0:depth], rest.astype(bf16))
        return nodes, total[NODE_ROWS:], value[0:FORCE_ROWS] + rest[0:FORCE_ROWS]

    def node_parts(out):
        parts = []
        for i in range(6):
            shifted = pltpu.roll(out[(6 + i) * sy : (7 + i) * sy], 1, 1) * not_first
            parts.append(out[i * sy : (i + 1) * sy] + shifted)
        rim = out[12 * sy : 12 * sy + 8] + pltpu.roll(out[12 * sy + 8 : 12 * sy + 16], 1, 1) * not_first
        return parts, rim

    return base, out_base, not_last, not_first, corner_tiles, weights, scaled, apply, node_parts


def element_layer(sizes, tools, edge, stiff_edge, mass_rows, stiff_out, mass_out, pair, layer):
    cols, sx, sy, sz = sizes
    _, _, not_last, _, corner_tiles, weights, scaled, apply, node_parts = tools

    def edge_tiles(k, layer):
        plain = stiff_edge[pl.ds((layer + 1) * SLAB, SLAB), :]
        cut = plain * jnp.concatenate([not_last, not_last], 0)
        tiles = []
        for a in range(2):
            tile = edge[pl.ds(((layer + 1 + a) * cols + k) * SLAB, SLAB), :]
            tiles.append(tile * plain)
            tiles.append(pltpu.roll(tile, sz - 1, 1) * cut)
        return tiles

    inner = 0 <= layer < sx
    columns = []
    kept = []
    for c in range(2):
        k = pair * 2 + c
        tiles = corner_tiles(k, layer)
        kept.append(tiles)
        columns.append(jnp.concatenate(scaled(tiles, layer) + edge_tiles(k, layer), 0))
    out, forces, doubled = apply(columns, NODE_ROWS + FORCE_ROWS if inner else NODE_ROWS, FORCE_ROWS + EDGE)
    results = []
    for c in range(2):
        k = pair * 2 + c
        if inner:
            work = forces[:, c * sz : (c + 1) * sz] * doubled[:, c * sz : (c + 1) * sz]
            energy = 0.0
            square = [0.0, 0.0]
            for alpha in range(24):
                q = (alpha // 3) % 2
                tile = kept[c][alpha]
                energy = energy + work[alpha * sy : (alpha + 1) * sy]
                square[q] = square[q] + tile * tile
            at = (k * sx + layer) * sy
            mass = mass_rows[pl.ds((layer + 1) * SLAB + 1, sy), :]
            stiff_out[pl.ds(at, sy), :] = energy * (3.0 / weights(layer)[0])
            mass_out[pl.ds(at, sy), :] = mass * (square[0] + square[1] * not_last)
        results.append(node_parts(out[:, c * sz : (c + 1) * sz]))
    return results


def store_parts(sy, ref, k, result):
    parts, rim = result
    for i, tile in enumerate(parts + [rim]):
        ref[pl.ds((k * 7 + i) * sy, sy), :] = tile


def load_parts(sy, ref, k):
    tiles = [ref[pl.ds((k * 7 + i) * sy, sy), :] for i in range(7)]
    return tiles[0:6], tiles[6]


def unpackers(sizes, tools, basis, edge, stiff, stiff_edge, mass_rows, scale):
    cols, sx, sy, sz = sizes
    slabs = cols * 3
    block = slabs * sx * sy
    plane = sx * sy
    field = block + slabs * sy
    n = slabs * sx
    span = sy + 1
    base = tools[0]

    def unpack(layer, source, low, high, at):
        low_ref, low_at = low
        high_ref, high_at = high
        for k in range(cols):
            for d in range(3):
                basis[pl.ds(base(layer, k, d), sy), :] = source[pl.ds(((k * 3 + d) * sx + at) * sy, sy), :]
        basis[pl.ds(base(layer, 0, 0) + sy, slabs, stride=span), :] = high_ref[pl.ds(high_at + at, slabs, stride=sx), :]
        for d in range(3):
            start = (layer + 1) * cols * SLAB + d * 4
            pick = d * sx + at
            edge[pl.ds(start, cols, stride=SLAB), :] = low_ref[pl.ds(low_at + pick, cols, stride=3 * sx), :]
            edge[pl.ds(start + 1, cols, stride=SLAB), :] = source[pl.ds(pick * sy, cols, stride=3 * sx * sy), :]
            edge[pl.ds(start + 2, cols, stride=SLAB), :] = high_ref[pl.ds(high_at + pick, cols, stride=3 * sx), :]
            edge[pl.ds(start + 3, cols, stride=SLAB), :] = high_ref[pl.ds(high_at + n + pick, cols, stride=3 * sx), :]

    def unpack_fields(layer, source, low, high, at):
        low_ref, low_at = low
        high_ref, high_at = high
        index = layer + 1
        stiff[pl.ds(index * sy, sy), :] = source[pl.ds(field + at * sy, sy), :]
        before = low_ref[pl.ds(low_at + n + at, 1), :]
        after = high_ref[pl.ds(high_at + 3 * n + at, 1), :]
        for j in range(4):
            row = before if j < 2 else after
            stiff_edge[pl.ds(index * SLAB + j, 3, stride=4), :] = jnp.broadcast_to(row, (3, sz))
        mass_rows[pl.ds(index * SLAB, 1), :] = low_ref[pl.ds(low_at + n + sx + at, 1), :]
        mass_rows[pl.ds(index * SLAB + 1, sy), :] = source[pl.ds(field + plane + at * sy, sy), :]
        mass_rows[pl.ds(index * SLAB + 1 + sy, 1), :] = high_ref[pl.ds(high_at + 3 * n + sx + at, 1), :]

    def unpack_prev(layer, source, high, at, stride, start):
        high_ref, high_at = high
        for k in range(cols):
            for d in range(3):
                basis[pl.ds(base(layer, 3 * cols + k, d), sy), :] = source[
                    pl.ds(start + ((k * 3 + d) * stride + at) * sy, sy), :
                ]
        basis[pl.ds(base(layer, 3 * cols, 0) + sy, slabs, stride=span), :] = high_ref[
            pl.ds(high_at + 2 * n + at, slabs, stride=sx), :
        ]

    def unpack_scale(layer, source, high, at):
        high_ref, high_at = high
        for d in range(3):
            scale[pl.ds((layer * 3 + d) * SLAB, sy), :] = source[pl.ds(field + 2 * plane + (d * sx + at) * sy, sy), :]
        scale[pl.ds(layer * 3 * SLAB + sy, 3, stride=SLAB), :] = high_ref[pl.ds(high_at + 3 * n + 2 * sx + at, 3, stride=sx), :]

    return unpack, unpack_fields, unpack_prev, unpack_scale


def early_kernel(
    sizes, own, prev_free, from_low, from_high, op_high, op_low,
    basis, edge, stiff, stiff_edge, mass_rows, scale, stiff_out, mass_out, parts_out, prev_parts,
):
    cols, sx, sy, sz = sizes
    tools = helpers(sizes, basis, stiff, op_high, op_low)
    _, _, _, _, corner_tiles, _, scaled, apply, node_parts = tools
    unpack, unpack_fields, unpack_prev, unpack_scale = unpackers(
        sizes, tools, basis, edge, stiff, stiff_edge, mass_rows, scale
    )
    edge[...] = jnp.zeros(edge.shape, f32)
    stiff_edge[...] = jnp.zeros(stiff_edge.shape, f32)
    low = (from_low, 0)
    high = (from_high, 0)
    for layer in range(sx):
        unpack(layer, own, low, high, layer)
        unpack_fields(layer, own, low, high, layer)
        unpack_prev(layer, prev_free, high, layer, sx, 0)
        unpack_scale(layer, own, high, layer)
    for layer in range(sx - 1):
        for pair in range(cols // 2):
            results = element_layer(sizes, tools, edge, stiff_edge, mass_rows, stiff_out, mass_out, pair, layer)
            for c in range(2):
                store_parts(sy, parts_out, layer * cols + pair * 2 + c, results[c])
        for pair in range(cols // 2):
            ks = [3 * cols + pair * 2 + c for c in range(2)]
            out = apply([jnp.concatenate(scaled(corner_tiles(k, layer), layer), 0) for k in ks], NODE_ROWS, FORCE_ROWS)[0]
            for c in range(2):
                store_parts(sy, prev_parts, layer * cols + pair * 2 + c, node_parts(out[:, c * sz : (c + 1) * sz]))


def current_kernel(
    sizes, place, pair_a, pair_b, corner_a, corner_b, op_high, op_low, parts_in,
    basis_in, edge_in, stiff_in, stiff_edge_in, mass_in, scale_in, energy_in, square_in,
    basis, edge, stiff, stiff_edge, mass_rows, scale, stiff_out, mass_out,
    applied, a_out, b_out, share_out, lumped,
    above, below,
):
    cols, sx, sy, sz = sizes
    low_rows = -(-(cols * 3 * sx + 2 * sx) // 8) * 8
    block = cols * 3 * sx * sy
    tools = helpers(sizes, basis, stiff, op_high, op_low)
    base, out_base, _, not_first, _, _, _, _, _ = tools
    unpack, unpack_fields, unpack_prev, unpack_scale = unpackers(
        sizes, tools, basis, edge, stiff, stiff_edge, mass_rows, scale
    )

    def unpack_sides(lower, lower_corner, upper, upper_corner):
        lower_high = (lower_corner, low_rows)
        unpack(-1, lower, (lower_corner, 0), lower_high, sx - 1)
        unpack_fields(-1, lower, (lower_corner, 0), lower_high, sx - 1)
        upper_high = (upper_corner, low_rows)
        for step in range(2):
            unpack(sx + step, upper, (upper_corner, 0), upper_high, step)
        unpack_fields(sx, upper, (upper_corner, 0), upper_high, 0)
        unpack_prev(sx, upper, upper_high, 0, 1, block)
        unpack_scale(sx, upper, upper_high, 0)

    @pl.when(place[0] == 1)
    def _():
        unpack_sides(pair_a, corner_a, pair_b, corner_b)

    @pl.when(place[0] == 0)
    def _():
        unpack_sides(pair_b, corner_b, pair_a, corner_a)

    for layer in range(sx + 1):
        first = layer * SLAB
        second = first + SLAB
        mass_sum = mass_rows[pl.ds(first, SLAB), :] + mass_rows[pl.ds(second, SLAB), :]
        lumped[pl.ds(layer * SLAB, SLAB), :] = mass_sum
        inner = lumped[pl.ds(layer * SLAB, sy), :] + lumped[pl.ds(layer * SLAB + 1, sy), :]
        outer = lumped[pl.ds(layer * SLAB + sy, 1), :] + lumped[pl.ds(layer * SLAB + sy + 1, 1), :]
        lumped[pl.ds(layer * SLAB, sy), :] = inner + pltpu.roll(inner, 1, 1) * not_first
        outer = jnp.broadcast_to(outer, (8, sz))
        outer = outer + pltpu.roll(outer, 1, 1) * not_first
        lumped[pl.ds(layer * SLAB + sy, 1), :] = outer[0:1]

    above[...] = jnp.zeros(above.shape, f32)
    below[...] = jnp.zeros(below.shape, f32)

    def current_pair(pair):
        sums = [[0.0, 0.0], [0.0, 0.0]]
        tails = [None, None]
        for layer in range(-1, sx + 1):
            if 0 <= layer < sx - 1:
                results = [load_parts(sy, parts_in, layer * cols + pair * 2 + c) for c in range(2)]
            else:
                results = element_layer(sizes, tools, edge, stiff_edge, mass_rows, stiff_out, mass_out, pair, layer)
            for c in range(2):
                k = pair * 2 + c
                parts, rim = results[c]
                if layer >= 0:
                    before, rim_before = tails[c]
                    rim_sum = rim[0:3] + rim_before[3:6]
                    load = lumped[pl.ds(layer * SLAB, SLAB), :]
                    for d in range(3):
                        total = parts[d] + before[3 + d]
                        factor = scale[pl.ds((layer * 3 + d) * SLAB, SLAB), :]
                        a_value = factor[0:sy] * total
                        both = factor * load
                        b_value = both[0:sy] * basis[pl.ds(base(layer, k, d), sy), :]
                        b_rim = both[sy : sy + 1] * basis[pl.ds(base(layer, k, d) + sy, 1), :]
                        basis[pl.ds(base(layer, cols + k, d), sy), :] = a_value
                        basis[pl.ds(base(layer, cols + k, d) + sy, 1), :] = factor[sy : sy + 1] * rim_sum[d : d + 1]
                        basis[pl.ds(base(layer, 2 * cols + k, d), sy), :] = b_value
                        basis[pl.ds(base(layer, 2 * cols + k, d) + sy, 1), :] = b_rim
                        if layer < sx:
                            value = basis[pl.ds(base(layer, k, d), sy), :]
                            sums[c][0] = sums[c][0] + value * total
                            sums[c][1] = sums[c][1] + value * value * load[0:sy]
                            applied[pl.ds(out_base(layer, k, d), sy), :] = total
                            at = ((k * 3 + d) * sx + layer) * sy
                            a_out[pl.ds(at, sy), :] = a_value
                            b_out[pl.ds(at, sy), :] = b_value
                        else:
                            applied[pl.ds(out_base(layer, k, d), sy), :] = jnp.zeros((sy, sz), f32)
                        applied[pl.ds(out_base(layer, k, d) + sy, 1), :] = jnp.zeros((1, sz), f32)
                tails[c] = (parts, rim)
        for c in range(2):
            above[pl.ds(pair * 2 + c, 1), :] = jnp.sum(sums[c][0], 0, keepdims=True)
            below[pl.ds(pair * 2 + c, 1), :] = jnp.sum(sums[c][1], 0, keepdims=True)

    for pair in range(cols // 2):
        current_pair(pair)

    half = sz // 2
    rows = cols * sx * sy
    wide = lax.broadcasted_iota(jnp.int32, (rows, sz), 1)
    stiff_all = stiff_out[...]
    mass_all = mass_out[...]
    first = place[1] == 0
    stiff_half = jnp.where(first, pltpu.roll(stiff_all, half, 1), stiff_all)
    mass_half = jnp.where(first, mass_all, pltpu.roll(mass_all, half, 1))
    share_out[0:rows] = jnp.where(wide < half, stiff_half, mass_half)
    spot = lax.broadcasted_iota(jnp.int32, above.shape, 1)
    top = jnp.sum(above[...], 1, keepdims=True)
    bottom = jnp.sum(below[...], 1, keepdims=True)
    share_out[rows:] = jnp.where(spot == OTHER_TOP, top, 0.0) + jnp.where(spot == OTHER_TOP + 1, bottom, 0.0)


def gram_kernel(sizes, basis, stiff, lumped, op_high, op_low, prev_parts, applied_in, applied, gram_out):
    cols, sx, sy, sz = sizes
    width = 4 * cols
    span = sy + 1
    _, out_base, _, _, corner_tiles, _, scaled, apply, node_parts = helpers(sizes, basis, stiff, op_high, op_low)

    def other_pair(pair):
        tails = [None, None]
        for layer in range(sx):
            first = cols + pair * 2
            if first >= 3 * cols and layer < sx - 1:
                results = [load_parts(sy, prev_parts, layer * cols + first - 3 * cols + c) for c in range(2)]
            else:
                columns = [jnp.concatenate(scaled(corner_tiles(first + c, layer), layer), 0) for c in range(2)]
                out = apply(columns, NODE_ROWS, FORCE_ROWS)[0]
                results = [node_parts(out[:, c * sz : (c + 1) * sz]) for c in range(2)]
            for c in range(2):
                k = first + c
                parts, rim = results[c]
                ends = [(layer, parts[0:3], rim[0:3], tails[c])]
                if layer == sx - 1:
                    ends.append((sx, parts[3:6], rim[3:6], None))
                for at, values, row, before in ends:
                    for d in range(3):
                        value = values[d]
                        last = row[d : d + 1]
                        if before is not None:
                            value = value + before[0][3 + d]
                            last = last + before[1][3 + d : 4 + d]
                        applied[pl.ds(out_base(at, k, d), sy), :] = value
                        applied[pl.ds(out_base(at, k, d) + sy, 1), :] = last
                tails[c] = (parts, rim)

    for pair in range(3 * cols // 2):
        other_pair(pair)

    def contract(left, right):
        return lax.dot_general(left, right, (((1,), (1,)), ((), ())), preferred_element_type=f32)

    step = 3 * span

    def product(applied_values, basis_values):
        left_high, left_low = split(jnp.concatenate(basis_values, 1))
        right_high, right_low = split(jnp.concatenate(applied_values, 1))
        rows = left_high.shape[0]
        both = contract(jnp.concatenate([left_high, left_low], 0), right_high)
        return both[0:rows] + both[rows:] + contract(left_high, right_low)

    def gram_layer(layer, carry):
        counted = (layer < sx).astype(f32)
        for d in range(3):
            values = []
            others = []
            for y in range(sy + 1):
                value = basis[pl.ds(((layer + 1) * width * 3 + d) * span + y, width, stride=step), :]
                other = applied[pl.ds((layer * width * 3 + d) * span + y, width, stride=step), :]
                mass = lumped[pl.ds(layer * SLAB + y, 1), :] * counted
                values.append(value)
                others.append(jnp.concatenate([other, value * mass if y < sy else jnp.zeros_like(value)], 0))
            carry = carry + product(others, values)
        return carry

    both = lax.fori_loop(0, sx + 1, gram_layer, jnp.zeros((width, 2 * width), f32))
    gram_stiff = both[:, 0:width]
    gram_out[...] = jnp.zeros(gram_out.shape, f32)
    gram_out[:, 0:width] = gram_stiff
    gram_out[:, 64 : 64 + width] = both[:, width : 2 * width]


def finish_kernel(
    sizes, dof, place, gram, a_in, b_in, stiff_in, mass_in, other, stiff_gram, mass_gram, search, sensitivity
):
    cols, sx, sy, sz = sizes
    eye = (
        lax.broadcasted_iota(jnp.int32, (cols, cols), 0) == lax.broadcasted_iota(jnp.int32, (cols, cols), 1)
    ).astype(f32)
    top = gram[0:cols, 0:cols] * eye
    bottom = gram[0:cols, 64 : 64 + cols] * eye
    quotient = jnp.sum(top, 1, keepdims=True) / jnp.sum(bottom, 1, keepdims=True)
    quotient_row = jnp.sum(top, 0, keepdims=True) / jnp.sum(bottom, 0, keepdims=True)
    for at, out in ((0, stiff_gram), (64, mass_gram)):
        whole = gram[:, at : at + 4 * cols]
        rows = jnp.concatenate(
            [whole[0:cols], whole[cols : 2 * cols] - quotient * whole[2 * cols : 3 * cols], whole[3 * cols :]], 0
        )
        out[:, 0, :] = (1.0 / dof) * jnp.concatenate(
            [
                rows[:, 0:cols],
                rows[:, cols : 2 * cols] - quotient_row * rows[:, 2 * cols : 3 * cols],
                rows[:, 3 * cols :],
            ],
            1,
        )

    def weigh(value, total):
        squared = value * value
        powered = 1.0 / (squared * squared)
        factor = powered / (total * (1.0 / dof))
        return jnp.sum(powered, 0, keepdims=True), factor, factor * value

    overall, coefficient, weighted = weigh(quotient, jnp.sum(bottom, 1, keepdims=True))
    other_total = gram[0:cols, OTHER_TOP + 1 : OTHER_TOP + 2]
    other_sum, other_coefficient, other_weighted = weigh(gram[0:cols, OTHER_TOP : OTHER_TOP + 1] / other_total, other_total)
    half = sz // 2
    spot = lax.broadcasted_iota(jnp.int32, (cols, sz), 1)
    other_factor = jnp.where(spot < half, other_coefficient, -other_weighted)
    plane = sx * sy
    mine = 0.0
    received = 0.0
    for j in range(cols):
        here = pl.ds(j * 3 * plane, 3 * plane)
        value = a_in[here, :] - quotient[j : j + 1] * b_in[here, :]
        search[0, j] = value.reshape(3, sx, sy, sz)
        part = pl.ds(j * plane, plane)
        mine = mine + coefficient[j : j + 1] * stiff_in[part, :] - weighted[j : j + 1] * mass_in[part, :]
        received = received + other_factor[j : j + 1] * other[part, :]
    received = received + pltpu.roll(received, half, 1)
    mine = jnp.where(place[1] == 0, mine, pltpu.roll(mine, half, 1))
    total = (mine + received) / (overall + other_sum)
    sensitivity[...] = total[:, 0:half].reshape(sx, sy, half)


def pairs(axis, first):
    count = lax.axis_size(axis)
    steps = []
    for i in range(first, count - 1, 2):
        steps += [(i, i + 1), (i + 1, i)]
    return steps


def sum_over(value, axis):
    count = lax.axis_size(axis)
    if count & (count - 1):
        return lax.psum(value, axis)
    distance = 1
    while distance < count:
        value = value + lax.ppermute(value, axis, [(i, i ^ distance) for i in range(count)])
        distance *= 2
    return value


def near(value):
    return pltpu.with_memory_space_constraint(value, pltpu.VMEM)


def far(value):
    return pltpu.with_memory_space_constraint(value, pltpu.HBM)


def shards(current, previous, element_stiffness, preconditioner, modulus, density, solid, clamped):
    cols = current.shape[1]
    sx, sy, sz = modulus.shape
    sizes = (cols, sx, sy, sz)
    slabs = cols * 3
    n = slabs * sx
    block = n * sy
    dof = 3.0 * sx * sy * sz * lax.axis_size("bx") * lax.axis_size("by")

    def struct(*shape):
        return jax.ShapeDtypeStruct(shape, f32)

    def kept(*shape, dtype=f32):
        return pltpu.VMEM(shape, dtype)

    own_rows = block + slabs * sy + 5 * sx * sy
    up_rows = -(-(n + 2 * sx) // 8) * 8
    down_rows = -(-(3 * n + 5 * sx) // 8) * 8
    sources = (current, previous, modulus, density, solid, preconditioner, clamped)
    odd_y = (lax.axis_index("by") % 2).astype(jnp.int32)
    own, prev_free, message_a, message_b = pl.pallas_call(
        lambda *refs: prepare_kernel(sizes, *refs),
        in_specs=[pl.BlockSpec(memory_space=pltpu.SMEM)] + [pl.BlockSpec(memory_space=pltpu.HBM)] * len(sources),
        scratch_shapes=[pltpu.VMEM(x.shape, x.dtype) for x in sources] + [pltpu.SemaphoreType.DMA((len(sources),))],
        out_shape=(kept(own_rows, sz), kept(block, sz), kept(down_rows, sz), kept(down_rows, sz)),
        compiler_params=pltpu.CompilerParams(vmem_limit_bytes=12 << 20),
        name="prepare",
    )(odd_y.reshape(1), *[far(x) for x in sources])
    rows_a = lax.ppermute(message_a, "by", pairs("by", 0))
    rows_b = lax.ppermute(message_b, "by", pairs("by", 1))
    from_low = jnp.where(odd_y == 1, rows_a[:up_rows], rows_b[:up_rows])
    from_high = jnp.where(odd_y == 1, rows_b, rows_a)
    row_pick, col_pick, op_mask = operator_tables(sy)
    tables = (element_stiffness, jnp.asarray(row_pick, bf16), jnp.asarray(col_pick, bf16), jnp.asarray(op_mask, bf16))
    op_high, op_low = pl.pallas_call(
        operator_kernel,
        in_specs=[pl.BlockSpec(memory_space=pltpu.HBM)] * len(tables),
        out_shape=(kept(NODE_ROWS + FORCE_ROWS, FORCE_ROWS + EDGE, dtype=bf16),) * 2,
        scratch_shapes=[pltpu.VMEM(x.shape, x.dtype) for x in tables] + [pltpu.SemaphoreType.DMA((len(tables),))],
        compiler_params=pltpu.CompilerParams(vmem_limit_bytes=8 << 20),
        name="operator",
    )(*[far(x) for x in tables])
    pair_a = lax.ppermute(own, "bx", pairs("bx", 0))
    pair_b = lax.ppermute(own, "bx", pairs("bx", 1))
    corner = jnp.concatenate([from_low, from_high], 0)
    corner_a = lax.ppermute(corner, "bx", pairs("bx", 0))
    corner_b = lax.ppermute(corner, "bx", pairs("bx", 1))
    place = jnp.stack([lax.axis_index("bx") % 2, lax.axis_index("real")]).astype(jnp.int32)
    width = 4 * cols
    span = sy + 1
    energies = cols * sx * sy
    vmem = pl.BlockSpec(memory_space=pltpu.VMEM)
    smem = pl.BlockSpec(memory_space=pltpu.SMEM)
    low_limit = pltpu.CompilerParams(vmem_limit_bytes=16 << 20)
    state_shapes = (
        kept((sx + 3) * width * 3 * span, sz),
        kept((sx + 3) * cols * SLAB, sz),
        kept((sx + 2) * sy, sz),
        kept((sx + 2) * SLAB, sz),
        kept((sx + 2) * SLAB, sz),
        kept((sx + 1) * 3 * SLAB, sz),
        kept(energies, sz),
        kept(energies, sz),
    )
    parts_shape = kept((sx - 1) * cols * 7 * sy, sz)
    *state, parts, prev_parts = pl.pallas_call(
        lambda *refs: early_kernel(sizes, *refs),
        in_specs=[vmem] * 6,
        out_shape=state_shapes + (parts_shape, parts_shape),
        compiler_params=low_limit,
        name="early",
    )(*[near(x) for x in (own, prev_free, from_low, from_high, op_high, op_low)])
    basis, _, stiff, _, _, _, stiff_part, mass_part, applied, a_part, b_part, shared, lumped = pl.pallas_call(
        lambda *refs: current_kernel(sizes, *refs),
        in_specs=[smem] + [vmem] * 15,
        out_shape=state_shapes
        + (
            kept((sx + 1) * width * 3 * span, sz),
            kept(block, sz),
            kept(block, sz),
            kept(energies + 16, sz),
            kept((sx + 1) * SLAB, sz),
        ),
        input_output_aliases={8 + i: i for i in range(8)},
        scratch_shapes=[pltpu.VMEM((16, sz), f32), pltpu.VMEM((16, sz), f32)],
        compiler_params=low_limit,
        name="current",
    )(place, *[near(x) for x in (pair_a, pair_b, corner_a, corner_b, op_high, op_low, parts, *state)])
    count = lax.axis_size("real")
    other = lax.ppermute(shared, "real", [(i, (i + 1) % count) for i in range(count)])
    _, gram = pl.pallas_call(
        lambda *refs: gram_kernel(sizes, *refs),
        in_specs=[vmem] * 7,
        out_shape=(kept((sx + 1) * width * 3 * span, sz), kept(width, 128)),
        input_output_aliases={6: 0},
        compiler_params=pltpu.CompilerParams(vmem_limit_bytes=16 << 20),
        name="gram",
    )(*[near(x) for x in (basis, stiff, lumped, op_high, op_low, prev_parts, applied)])
    gram = jnp.concatenate([gram[0:16] + other[energies:], gram[16:]], 0)
    gram = sum_over(sum_over(gram, "bx"), "by")
    stiff_gram, mass_gram, search, sensitivity = pl.pallas_call(
        lambda *refs: finish_kernel(sizes, dof, *refs),
        in_specs=[smem] + [vmem] * 6,
        out_shape=(
            struct(3 * cols, 1, 3 * cols),
            struct(3 * cols, 1, 3 * cols),
            struct(1, cols, 3, sx, sy, sz),
            struct(sx, sy, sz // 2),
        ),
        compiler_params=pltpu.CompilerParams(vmem_limit_bytes=12 << 20),
        name="finish",
    )(place, *[near(x) for x in (gram, a_part, b_part, stiff_part, mass_part, other)])
    return jnp.swapaxes(stiff_gram, 0, 1), jnp.swapaxes(mass_gram, 0, 1), search, sensitivity


def solution(mesh):
    in_specs = (
        P("real", None, None, "bx", "by", None),
        P("real", None, None, "bx", "by", None),
        P(),
        P("real", None, "bx", "by", None),
        P("bx", "by", None),
        P("bx", "by", None),
        P("real", "bx", "by", None),
        P("bx", "by"),
    )
    out_specs = (
        P("real", None, None),
        P("real", None, None),
        P("real", None, None, "bx", "by", None),
        P("bx", "by", "real"),
    )
    return jax.shard_map(shards, mesh=mesh, in_specs=in_specs, out_specs=out_specs, check_vma=False)
```

```python
import numpy as np
import jax
import jax.numpy as jnp
from jax import lax
from jax.experimental import pallas as pl
from jax.experimental.pallas import tpu as pltpu
from jax.sharding import PartitionSpec as P

f32 = jnp.float32
bf16 = jnp.bfloat16
SLAB = 16
NODE_ROWS = 112
FORCE_ROWS = 192
OTHER_TOP = 60
EDGE = 64


def operator_tables(rows):
    row_pick = np.zeros((2, NODE_ROWS + FORCE_ROWS, 24), np.float32)
    col_pick = np.zeros((24, FORCE_ROWS + EDGE), np.float32)
    col_y = np.full(FORCE_ROWS + EDGE, -99)
    for beta in range(24):
        for y in range(rows):
            col_pick[beta, beta * rows + y] = 1
            col_y[beta * rows + y] = y
    for a in range(2):
        for q in range(2):
            for d in range(3):
                for j in range(4):
                    k = FORCE_ROWS + (a * 2 + q) * 16 + d * 4 + j
                    col_pick[(4 * a + 2 * (j % 2) + q) * 3 + d, k] = 1
                    col_y[k] = -1 if j < 2 else rows
    mask = np.zeros((2, NODE_ROWS + FORCE_ROWS, FORCE_ROWS + EDGE), np.float32)
    for q in range(2):
        for a in range(2):
            for d in range(3):
                for y in range(rows + 1):
                    m = (q * 6 + a * 3 + d) * rows + y
                    if y == rows:
                        m = 12 * rows + q * 8 + a * 3 + d
                    for b in range(2):
                        row_pick[b, m, (4 * a + 2 * b + q) * 3 + d] = 1
                        mask[b, m] = col_y == y - b
    for alpha in range(24):
        for y in range(rows):
            m = NODE_ROWS + alpha * rows + y
            row_pick[0, m, alpha] = 1
            mask[0, m, :FORCE_ROWS] = col_y[:FORCE_ROWS] == y
    return row_pick, col_pick, mask


def split(value):
    high = value.astype(bf16)
    return high, (value - high.astype(f32)).astype(bf16)


def dot(left, right):
    return jnp.dot(left, right, preferred_element_type=f32)


def fetch(sources, buffers, arrived):
    copies = [pltpu.make_async_copy(source, buffer, arrived.at[i]) for i, (source, buffer) in enumerate(zip(sources, buffers))]
    for copy in copies:
        copy.start()
    for copy in copies:
        copy.wait()
    return buffers


def operator_kernel(*refs):
    high_out, low_out = refs[4:6]
    matrix, row_pick, col_pick, mask = fetch(refs[0:4], refs[6:10], refs[10])
    high, low = split(matrix[...])
    for part, out in ((high, high_out), (low, low_out)):
        total = 0.0
        for b in range(2):
            picked = dot(row_pick[b], part).astype(bf16)
            total = total + dot(picked, col_pick[...]) * mask[b].astype(f32)
        out[...] = total.astype(bf16)


def prepare_kernel(sizes, odd, *refs):
    own, prev_free, message_a, message_b = refs[7:11]
    cur, prev, modulus, density, solid, precond, clamped = fetch(refs[0:7], refs[11:18], refs[18])
    cols, sx, sy, sz = sizes
    slabs = cols * 3
    block = slabs * sx * sy
    held = clamped[...].astype(f32)
    eye = (lax.broadcasted_iota(jnp.int32, (sy, sy), 0) == lax.broadcasted_iota(jnp.int32, (sy, sy), 1)).astype(f32)
    bottom = (lax.broadcasted_iota(jnp.int32, (sy, sz), 1) == 0).astype(f32)
    planes = []
    for x in range(sx):
        column = jnp.sum(jnp.broadcast_to(held[x : x + 1], (sy, sy)) * eye, 1, keepdims=True)
        planes.append((1.0 - column * bottom)[None])
    free = jnp.concatenate(planes, 0)
    share = solid[0].astype(f32)
    own[0:block] = (cur[0] * free[None, None]).reshape(block, sz)
    masked = prev[0] * free[None, None]
    prev_free[...] = masked.reshape(block, sz)
    own[block : block + slabs * sy] = masked[:, :, 0].reshape(slabs * sy, sz)
    field = block + slabs * sy
    plane = sx * sy
    own[field : field + plane] = (modulus[...] * (0.02 + 0.98 * share)).reshape(plane, sz)
    own[field + plane : field + 2 * plane] = (density[...] * (0.1 + 0.9 * share) * 0.125).reshape(plane, sz)
    own[field + 2 * plane : field + 5 * plane] = (precond[0] * free[None]).reshape(3 * plane, sz)
    n = slabs * sx

    def fill(up, down):
        up[0:n] = own[pl.ds(sy - 1, n, stride=sy), :]
        up[n : n + 2 * sx] = own[pl.ds(field + sy - 1, 2 * sx, stride=sy), :]
        down[0:n] = own[pl.ds(0, n, stride=sy), :]
        down[n : 2 * n] = own[pl.ds(1, n, stride=sy), :]
        down[2 * n : 3 * n] = prev_free[pl.ds(0, n, stride=sy), :]
        down[3 * n : 3 * n + 5 * sx] = own[pl.ds(field, 5 * sx, stride=sy), :]

    @pl.when(odd[0] == 1)
    def _():
        fill(message_b, message_a)

    @pl.when(odd[0] == 0)
    def _():
        fill(message_a, message_b)


def helpers(sizes, basis, stiff, op_high, op_low):
    cols, _, sy, sz = sizes
    width = 4 * cols
    span = sy + 1
    lane = lax.broadcasted_iota(jnp.int32, (8, sz), 1)
    not_last = (lane < sz - 1).astype(f32)
    not_first = (lane > 0).astype(f32)

    def base(layer, k, d):
        return (((layer + 1) * width + k) * 3 + d) * span

    def out_base(layer, k, d):
        return ((layer * width + k) * 3 + d) * span

    def corner_tiles(k, layer):
        tiles = []
        for a in range(2):
            for b in range(2):
                near = [basis[pl.ds(base(layer + a, k, d) + b, sy), :] for d in range(3)]
                tiles += near
                tiles += [pltpu.roll(tile, sz - 1, 1) for tile in near]
        return tiles

    def weights(layer):
        plain = stiff[pl.ds((layer + 1) * sy, sy), :]
        return plain, plain * not_last

    def scaled(tiles, layer):
        plain, cut = weights(layer)
        return [tile * (cut if (i // 3) % 2 else plain) for i, tile in enumerate(tiles)]

    def apply(columns, rows, depth):
        value = jnp.concatenate(columns, 1)
        high = value.astype(bf16)
        rest = value - high.astype(f32)
        both = dot(jnp.concatenate([op_high[0:rows, 0:depth], op_low[0:rows, 0:depth]], 0), high)
        total = both[0:rows] + both[rows:]
        nodes = total[0:NODE_ROWS] + dot(op_high[0:NODE_ROWS, 0:depth], rest.astype(bf16))
        return nodes, total[NODE_ROWS:], value[0:FORCE_ROWS] + rest[0:FORCE_ROWS]

    def node_parts(out):
        parts = []
        for i in range(6):
            shifted = pltpu.roll(out[(6 + i) * sy : (7 + i) * sy], 1, 1) * not_first
            parts.append(out[i * sy : (i + 1) * sy] + shifted)
        rim = out[12 * sy : 12 * sy + 8] + pltpu.roll(out[12 * sy + 8 : 12 * sy + 16], 1, 1) * not_first
        return parts, rim

    return base, out_base, not_last, not_first, corner_tiles, weights, scaled, apply, node_parts


def element_layer(sizes, tools, edge, stiff_edge, mass_rows, stiff_out, mass_out, pair, layer):
    cols, sx, sy, sz = sizes
    _, _, not_last, _, corner_tiles, weights, scaled, apply, node_parts = tools

    def edge_tiles(k, layer):
        plain = stiff_edge[pl.ds((layer + 1) * SLAB, SLAB), :]
        cut = plain * jnp.concatenate([not_last, not_last], 0)
        tiles = []
        for a in range(2):
            tile = edge[pl.ds(((layer + 1 + a) * cols + k) * SLAB, SLAB), :]
            tiles.append(tile * plain)
            tiles.append(pltpu.roll(tile, sz - 1, 1) * cut)
        return tiles

    inner = 0 <= layer < sx
    columns = []
    kept = []
    for c in range(2):
        k = pair * 2 + c
        tiles = corner_tiles(k, layer)
        kept.append(tiles)
        columns.append(jnp.concatenate(scaled(tiles, layer) + edge_tiles(k, layer), 0))
    out, forces, doubled = apply(columns, NODE_ROWS + FORCE_ROWS if inner else NODE_ROWS, FORCE_ROWS + EDGE)
    results = []
    for c in range(2):
        k = pair * 2 + c
        if inner:
            work = forces[:, c * sz : (c + 1) * sz] * doubled[:, c * sz : (c + 1) * sz]
            energy = 0.0
            square = [0.0, 0.0]
            for alpha in range(24):
                q = (alpha // 3) % 2
                tile = kept[c][alpha]
                energy = energy + work[alpha * sy : (alpha + 1) * sy]
                square[q] = square[q] + tile * tile
            at = (k * sx + layer) * sy
            mass = mass_rows[pl.ds((layer + 1) * SLAB + 1, sy), :]
            stiff_out[pl.ds(at, sy), :] = energy * (3.0 / weights(layer)[0])
            mass_out[pl.ds(at, sy), :] = mass * (square[0] + square[1] * not_last)
        results.append(node_parts(out[:, c * sz : (c + 1) * sz]))
    return results


def store_parts(sy, ref, k, result):
    parts, rim = result
    for i, tile in enumerate(parts + [rim]):
        ref[pl.ds((k * 7 + i) * sy, sy), :] = tile


def load_parts(sy, ref, k):
    tiles = [ref[pl.ds((k * 7 + i) * sy, sy), :] for i in range(7)]
    return tiles[0:6], tiles[6]


def unpackers(sizes, tools, basis, edge, stiff, stiff_edge, mass_rows, scale):
    cols, sx, sy, sz = sizes
    slabs = cols * 3
    block = slabs * sx * sy
    plane = sx * sy
    field = block + slabs * sy
    n = slabs * sx
    span = sy + 1
    base = tools[0]

    def unpack(layer, source, low, high, at):
        low_ref, low_at = low
        high_ref, high_at = high
        for k in range(cols):
            for d in range(3):
                basis[pl.ds(base(layer, k, d), sy), :] = source[pl.ds(((k * 3 + d) * sx + at) * sy, sy), :]
        basis[pl.ds(base(layer, 0, 0) + sy, slabs, stride=span), :] = high_ref[pl.ds(high_at + at, slabs, stride=sx), :]
        for d in range(3):
            start = (layer + 1) * cols * SLAB + d * 4
            pick = d * sx + at
            edge[pl.ds(start, cols, stride=SLAB), :] = low_ref[pl.ds(low_at + pick, cols, stride=3 * sx), :]
            edge[pl.ds(start + 1, cols, stride=SLAB), :] = source[pl.ds(pick * sy, cols, stride=3 * sx * sy), :]
            edge[pl.ds(start + 2, cols, stride=SLAB), :] = high_ref[pl.ds(high_at + pick, cols, stride=3 * sx), :]
            edge[pl.ds(start + 3, cols, stride=SLAB), :] = high_ref[pl.ds(high_at + n + pick, cols, stride=3 * sx), :]

    def unpack_fields(layer, source, low, high, at):
        low_ref, low_at = low
        high_ref, high_at = high
        index = layer + 1
        stiff[pl.ds(index * sy, sy), :] = source[pl.ds(field + at * sy, sy), :]
        before = low_ref[pl.ds(low_at + n + at, 1), :]
        after = high_ref[pl.ds(high_at + 3 * n + at, 1), :]
        for j in range(4):
            row = before if j < 2 else after
            stiff_edge[pl.ds(index * SLAB + j, 3, stride=4), :] = jnp.broadcast_to(row, (3, sz))
        mass_rows[pl.ds(index * SLAB, 1), :] = low_ref[pl.ds(low_at + n + sx + at, 1), :]
        mass_rows[pl.ds(index * SLAB + 1, sy), :] = source[pl.ds(field + plane + at * sy, sy), :]
        mass_rows[pl.ds(index * SLAB + 1 + sy, 1), :] = high_ref[pl.ds(high_at + 3 * n + sx + at, 1), :]

    def unpack_prev(layer, source, high, at, stride, start):
        high_ref, high_at = high
        for k in range(cols):
            for d in range(3):
                basis[pl.ds(base(layer, 3 * cols + k, d), sy), :] = source[
                    pl.ds(start + ((k * 3 + d) * stride + at) * sy, sy), :
                ]
        basis[pl.ds(base(layer, 3 * cols, 0) + sy, slabs, stride=span), :] = high_ref[
            pl.ds(high_at + 2 * n + at, slabs, stride=sx), :
        ]

    def unpack_scale(layer, source, high, at):
        high_ref, high_at = high
        for d in range(3):
            scale[pl.ds((layer * 3 + d) * SLAB, sy), :] = source[pl.ds(field + 2 * plane + (d * sx + at) * sy, sy), :]
        scale[pl.ds(layer * 3 * SLAB + sy, 3, stride=SLAB), :] = high_ref[pl.ds(high_at + 3 * n + 2 * sx + at, 3, stride=sx), :]

    return unpack, unpack_fields, unpack_prev, unpack_scale


def early_kernel(
    sizes, own, prev_free, from_low, from_high, op_high, op_low,
    basis, edge, stiff, stiff_edge, mass_rows, scale, stiff_out, mass_out, parts_out, prev_parts,
):
    cols, sx, sy, sz = sizes
    tools = helpers(sizes, basis, stiff, op_high, op_low)
    _, _, _, _, corner_tiles, _, scaled, apply, node_parts = tools
    unpack, unpack_fields, unpack_prev, unpack_scale = unpackers(
        sizes, tools, basis, edge, stiff, stiff_edge, mass_rows, scale
    )
    edge[...] = jnp.zeros(edge.shape, f32)
    stiff_edge[...] = jnp.zeros(stiff_edge.shape, f32)
    low = (from_low, 0)
    high = (from_high, 0)
    for layer in range(sx):
        unpack(layer, own, low, high, layer)
        unpack_fields(layer, own, low, high, layer)
        unpack_prev(layer, prev_free, high, layer, sx, 0)
        unpack_scale(layer, own, high, layer)
    for layer in range(sx - 1):
        for pair in range(cols // 2):
            results = element_layer(sizes, tools, edge, stiff_edge, mass_rows, stiff_out, mass_out, pair, layer)
            for c in range(2):
                store_parts(sy, parts_out, layer * cols + pair * 2 + c, results[c])
        for pair in range(cols // 2):
            ks = [3 * cols + pair * 2 + c for c in range(2)]
            out = apply([jnp.concatenate(scaled(corner_tiles(k, layer), layer), 0) for k in ks], NODE_ROWS, FORCE_ROWS)[0]
            for c in range(2):
                store_parts(sy, prev_parts, layer * cols + pair * 2 + c, node_parts(out[:, c * sz : (c + 1) * sz]))


def current_kernel(
    sizes, place, pair_a, pair_b, corner_a, corner_b, op_high, op_low, parts_in,
    basis_in, edge_in, stiff_in, stiff_edge_in, mass_in, scale_in, energy_in, square_in,
    basis, edge, stiff, stiff_edge, mass_rows, scale, stiff_out, mass_out,
    applied, a_out, b_out, share_out, lumped,
    above, below,
):
    cols, sx, sy, sz = sizes
    low_rows = -(-(cols * 3 * sx + 2 * sx) // 8) * 8
    block = cols * 3 * sx * sy
    tools = helpers(sizes, basis, stiff, op_high, op_low)
    base, out_base, _, not_first, _, _, _, _, _ = tools
    unpack, unpack_fields, unpack_prev, unpack_scale = unpackers(
        sizes, tools, basis, edge, stiff, stiff_edge, mass_rows, scale
    )

    def unpack_sides(lower, lower_corner, upper, upper_corner):
        lower_high = (lower_corner, low_rows)
        unpack(-1, lower, (lower_corner, 0), lower_high, sx - 1)
        unpack_fields(-1, lower, (lower_corner, 0), lower_high, sx - 1)
        upper_high = (upper_corner, low_rows)
        for step in range(2):
            unpack(sx + step, upper, (upper_corner, 0), upper_high, step)
        unpack_fields(sx, upper, (upper_corner, 0), upper_high, 0)
        unpack_prev(sx, upper, upper_high, 0, 1, block)
        unpack_scale(sx, upper, upper_high, 0)

    @pl.when(place[0] == 1)
    def _():
        unpack_sides(pair_a, corner_a, pair_b, corner_b)

    @pl.when(place[0] == 0)
    def _():
        unpack_sides(pair_b, corner_b, pair_a, corner_a)

    for layer in range(sx + 1):
        first = layer * SLAB
        second = first + SLAB
        mass_sum = mass_rows[pl.ds(first, SLAB), :] + mass_rows[pl.ds(second, SLAB), :]
        lumped[pl.ds(layer * SLAB, SLAB), :] = mass_sum
        inner = lumped[pl.ds(layer * SLAB, sy), :] + lumped[pl.ds(layer * SLAB + 1, sy), :]
        outer = lumped[pl.ds(layer * SLAB + sy, 1), :] + lumped[pl.ds(layer * SLAB + sy + 1, 1), :]
        lumped[pl.ds(layer * SLAB, sy), :] = inner + pltpu.roll(inner, 1, 1) * not_first
        outer = jnp.broadcast_to(outer, (8, sz))
        outer = outer + pltpu.roll(outer, 1, 1) * not_first
        lumped[pl.ds(layer * SLAB + sy, 1), :] = outer[0:1]

    above[...] = jnp.zeros(above.shape, f32)
    below[...] = jnp.zeros(below.shape, f32)

    def current_pair(pair):
        sums = [[0.0, 0.0], [0.0, 0.0]]
        tails = [None, None]
        for layer in range(-1, sx + 1):
            if 0 <= layer < sx - 1:
                results = [load_parts(sy, parts_in, layer * cols + pair * 2 + c) for c in range(2)]
            else:
                results = element_layer(sizes, tools, edge, stiff_edge, mass_rows, stiff_out, mass_out, pair, layer)
            for c in range(2):
                k = pair * 2 + c
                parts, rim = results[c]
                if layer >= 0:
                    before, rim_before = tails[c]
                    rim_sum = rim[0:3] + rim_before[3:6]
                    load = lumped[pl.ds(layer * SLAB, SLAB), :]
                    for d in range(3):
                        total = parts[d] + before[3 + d]
                        factor = scale[pl.ds((layer * 3 + d) * SLAB, SLAB), :]
                        a_value = factor[0:sy] * total
                        both = factor * load
                        b_value = both[0:sy] * basis[pl.ds(base(layer, k, d), sy), :]
                        b_rim = both[sy : sy + 1] * basis[pl.ds(base(layer, k, d) + sy, 1), :]
                        basis[pl.ds(base(layer, cols + k, d), sy), :] = a_value
                        basis[pl.ds(base(layer, cols + k, d) + sy, 1), :] = factor[sy : sy + 1] * rim_sum[d : d + 1]
                        basis[pl.ds(base(layer, 2 * cols + k, d), sy), :] = b_value
                        basis[pl.ds(base(layer, 2 * cols + k, d) + sy, 1), :] = b_rim
                        if layer < sx:
                            value = basis[pl.ds(base(layer, k, d), sy), :]
                            sums[c][0] = sums[c][0] + value * total
                            sums[c][1] = sums[c][1] + value * value * load[0:sy]
                            applied[pl.ds(out_base(layer, k, d), sy), :] = total
                            at = ((k * 3 + d) * sx + layer) * sy
                            a_out[pl.ds(at, sy), :] = a_value
                            b_out[pl.ds(at, sy), :] = b_value
                        else:
                            applied[pl.ds(out_base(layer, k, d), sy), :] = jnp.zeros((sy, sz), f32)
                        applied[pl.ds(out_base(layer, k, d) + sy, 1), :] = jnp.zeros((1, sz), f32)
                tails[c] = (parts, rim)
        for c in range(2):
            above[pl.ds(pair * 2 + c, 1), :] = jnp.sum(sums[c][0], 0, keepdims=True)
            below[pl.ds(pair * 2 + c, 1), :] = jnp.sum(sums[c][1], 0, keepdims=True)

    for pair in range(cols // 2):
        current_pair(pair)

    half = sz // 2
    rows = cols * sx * sy
    wide = lax.broadcasted_iota(jnp.int32, (rows, sz), 1)
    stiff_all = stiff_out[...]
    mass_all = mass_out[...]
    first = place[1] == 0
    stiff_half = jnp.where(first, pltpu.roll(stiff_all, half, 1), stiff_all)
    mass_half = jnp.where(first, mass_all, pltpu.roll(mass_all, half, 1))
    share_out[0:rows] = jnp.where(wide < half, stiff_half, mass_half)
    spot = lax.broadcasted_iota(jnp.int32, above.shape, 1)
    top = jnp.sum(above[...], 1, keepdims=True)
    bottom = jnp.sum(below[...], 1, keepdims=True)
    share_out[rows:] = jnp.where(spot == OTHER_TOP, top, 0.0) + jnp.where(spot == OTHER_TOP + 1, bottom, 0.0)


def gram_kernel(sizes, basis, stiff, lumped, op_high, op_low, prev_parts, applied_in, applied, gram_out):
    cols, sx, sy, sz = sizes
    width = 4 * cols
    span = sy + 1
    _, out_base, _, _, corner_tiles, _, scaled, apply, node_parts = helpers(sizes, basis, stiff, op_high, op_low)

    def other_pair(pair):
        tails = [None, None]
        for layer in range(sx):
            first = cols + pair * 2
            if first >= 3 * cols and layer < sx - 1:
                results = [load_parts(sy, prev_parts, layer * cols + first - 3 * cols + c) for c in range(2)]
            else:
                columns = [jnp.concatenate(scaled(corner_tiles(first + c, layer), layer), 0) for c in range(2)]
                out = apply(columns, NODE_ROWS, FORCE_ROWS)[0]
                results = [node_parts(out[:, c * sz : (c + 1) * sz]) for c in range(2)]
            for c in range(2):
                k = first + c
                parts, rim = results[c]
                ends = [(layer, parts[0:3], rim[0:3], tails[c])]
                if layer == sx - 1:
                    ends.append((sx, parts[3:6], rim[3:6], None))
                for at, values, row, before in ends:
                    for d in range(3):
                        value = values[d]
                        last = row[d : d + 1]
                        if before is not None:
                            value = value + before[0][3 + d]
                            last = last + before[1][3 + d : 4 + d]
                        applied[pl.ds(out_base(at, k, d), sy), :] = value
                        applied[pl.ds(out_base(at, k, d) + sy, 1), :] = last
                tails[c] = (parts, rim)

    for pair in range(3 * cols // 2):
        other_pair(pair)

    def contract(left, right):
        return lax.dot_general(left, right, (((1,), (1,)), ((), ())), preferred_element_type=f32)

    step = 3 * span

    def product(applied_values, basis_values):
        left_high, left_low = split(jnp.concatenate(basis_values, 1))
        right_high, right_low = split(jnp.concatenate(applied_values, 1))
        rows = left_high.shape[0]
        both = contract(jnp.concatenate([left_high, left_low], 0), right_high)
        return both[0:rows] + both[rows:] + contract(left_high, right_low)

    def gram_layer(layer, carry):
        counted = (layer < sx).astype(f32)
        for d in range(3):
            values = []
            others = []
            for y in range(sy + 1):
                value = basis[pl.ds(((layer + 1) * width * 3 + d) * span + y, width, stride=step), :]
                other = applied[pl.ds((layer * width * 3 + d) * span + y, width, stride=step), :]
                mass = lumped[pl.ds(layer * SLAB + y, 1), :] * counted
                values.append(value)
                others.append(jnp.concatenate([other, value * mass if y < sy else jnp.zeros_like(value)], 0))
            carry = carry + product(others, values)
        return carry

    both = lax.fori_loop(0, sx + 1, gram_layer, jnp.zeros((width, 2 * width), f32))
    gram_stiff = both[:, 0:width]
    one, two, three = cols, 2 * cols, 3 * cols
    empty = jnp.zeros((cols, 64 - 5 * cols), f32)
    first = []
    second = []
    for whole in (gram_stiff, both[:, width : 2 * width]):
        first += [whole[0:one], whole[two:three, two:three], empty]
        second += [whole[three:, three:], whole[one:two, one:], whole[two:three, three:], empty]
    gram_out[0:cols] = jnp.concatenate(first, 1)
    gram_out[cols : 2 * cols] = jnp.concatenate(second, 1)


def finish_kernel(
    sizes, dof, place, gram, a_in, b_in, stiff_in, mass_in, other, stiff_gram, mass_gram, search, sensitivity
):
    cols, sx, sy, sz = sizes
    eye = (
        lax.broadcasted_iota(jnp.int32, (cols, cols), 0) == lax.broadcasted_iota(jnp.int32, (cols, cols), 1)
    ).astype(f32)
    top = gram[0:cols, 0:cols] * eye
    bottom = gram[0:cols, 64 : 64 + cols] * eye
    quotient = jnp.sum(top, 1, keepdims=True) / jnp.sum(bottom, 1, keepdims=True)
    quotient_row = jnp.sum(top, 0, keepdims=True) / jnp.sum(bottom, 0, keepdims=True)
    for at, out in ((0, stiff_gram), (64, mass_gram)):
        first = gram[0:cols, at : at + 64]
        second = gram[cols : 2 * cols, at : at + 64]
        cc, ca, cb, cp, bb = [first[:, i * cols : (i + 1) * cols] for i in range(5)]
        pp, aa, ab, ap, bp = [second[:, i * cols : (i + 1) * cols] for i in range(5)]
        cross = ab * quotient_row
        blank = jnp.zeros((cols, cols), f32)
        tail = jnp.zeros((cols, sz - 3 * cols), f32)
        above = jnp.concatenate(
            [
                jnp.concatenate([blank, ca - cb * quotient_row, cp, tail], 1),
                jnp.concatenate([blank, -cross, ap - quotient * bp, tail], 1),
                jnp.zeros((sz - 2 * cols, sz), f32),
            ],
            0,
        )
        level = jnp.concatenate(
            [
                jnp.concatenate([cc, blank, blank], 1),
                jnp.concatenate([blank, aa + quotient * quotient_row * bb, blank], 1),
                jnp.concatenate([blank, blank, pp], 1),
            ],
            0,
        )
        full = level + (above + above.T)[0 : 3 * cols, 0 : 3 * cols]
        out[:, 0, :] = (1.0 / dof) * full

    def weigh(value, total):
        squared = value * value
        powered = 1.0 / (squared * squared)
        factor = powered / (total * (1.0 / dof))
        return jnp.sum(powered, 0, keepdims=True), factor, factor * value

    overall, coefficient, weighted = weigh(quotient, jnp.sum(bottom, 1, keepdims=True))
    other_total = gram[0:cols, OTHER_TOP + 1 : OTHER_TOP + 2]
    other_sum, other_coefficient, other_weighted = weigh(gram[0:cols, OTHER_TOP : OTHER_TOP + 1] / other_total, other_total)
    half = sz // 2
    spot = lax.broadcasted_iota(jnp.int32, (cols, sz), 1)
    other_factor = jnp.where(spot < half, other_coefficient, -other_weighted)
    plane = sx * sy
    mine = 0.0
    received = 0.0
    for j in range(cols):
        here = pl.ds(j * 3 * plane, 3 * plane)
        value = a_in[here, :] - quotient[j : j + 1] * b_in[here, :]
        search[0, j] = value.reshape(3, sx, sy, sz)
        part = pl.ds(j * plane, plane)
        mine = mine + coefficient[j : j + 1] * stiff_in[part, :] - weighted[j : j + 1] * mass_in[part, :]
        received = received + other_factor[j : j + 1] * other[part, :]
    received = received + pltpu.roll(received, half, 1)
    mine = jnp.where(place[1] == 0, mine, pltpu.roll(mine, half, 1))
    total = (mine + received) / (overall + other_sum)
    sensitivity[...] = total[:, 0:half].reshape(sx, sy, half)


def pairs(axis, first):
    count = lax.axis_size(axis)
    steps = []
    for i in range(first, count - 1, 2):
        steps += [(i, i + 1), (i + 1, i)]
    return steps


def sum_over(value, axis):
    count = lax.axis_size(axis)
    if count & (count - 1):
        return lax.psum(value, axis)
    distance = 1
    while distance < count:
        value = value + lax.ppermute(value, axis, [(i, i ^ distance) for i in range(count)])
        distance *= 2
    return value


def near(value):
    return pltpu.with_memory_space_constraint(value, pltpu.VMEM)


def far(value):
    return pltpu.with_memory_space_constraint(value, pltpu.HBM)


def shards(current, previous, element_stiffness, preconditioner, modulus, density, solid, clamped):
    cols = current.shape[1]
    sx, sy, sz = modulus.shape
    sizes = (cols, sx, sy, sz)
    slabs = cols * 3
    n = slabs * sx
    block = n * sy
    dof = 3.0 * sx * sy * sz * lax.axis_size("bx") * lax.axis_size("by")

    def struct(*shape):
        return jax.ShapeDtypeStruct(shape, f32)

    def kept(*shape, dtype=f32):
        return pltpu.VMEM(shape, dtype)

    own_rows = block + slabs * sy + 5 * sx * sy
    up_rows = -(-(n + 2 * sx) // 8) * 8
    down_rows = -(-(3 * n + 5 * sx) // 8) * 8
    sources = (current, previous, modulus, density, solid, preconditioner, clamped)
    odd_y = (lax.axis_index("by") % 2).astype(jnp.int32)
    own, prev_free, message_a, message_b = pl.pallas_call(
        lambda *refs: prepare_kernel(sizes, *refs),
        in_specs=[pl.BlockSpec(memory_space=pltpu.SMEM)] + [pl.BlockSpec(memory_space=pltpu.HBM)] * len(sources),
        scratch_shapes=[pltpu.VMEM(x.shape, x.dtype) for x in sources] + [pltpu.SemaphoreType.DMA((len(sources),))],
        out_shape=(kept(own_rows, sz), kept(block, sz), kept(down_rows, sz), kept(down_rows, sz)),
        compiler_params=pltpu.CompilerParams(vmem_limit_bytes=12 << 20),
        name="prepare",
    )(odd_y.reshape(1), *[far(x) for x in sources])
    rows_a = lax.ppermute(message_a, "by", pairs("by", 0))
    rows_b = lax.ppermute(message_b, "by", pairs("by", 1))
    from_low = jnp.where(odd_y == 1, rows_a[:up_rows], rows_b[:up_rows])
    from_high = jnp.where(odd_y == 1, rows_b, rows_a)
    row_pick, col_pick, op_mask = operator_tables(sy)
    tables = (element_stiffness, jnp.asarray(row_pick, bf16), jnp.asarray(col_pick, bf16), jnp.asarray(op_mask, bf16))
    op_high, op_low = pl.pallas_call(
        operator_kernel,
        in_specs=[pl.BlockSpec(memory_space=pltpu.HBM)] * len(tables),
        out_shape=(kept(NODE_ROWS + FORCE_ROWS, FORCE_ROWS + EDGE, dtype=bf16),) * 2,
        scratch_shapes=[pltpu.VMEM(x.shape, x.dtype) for x in tables] + [pltpu.SemaphoreType.DMA((len(tables),))],
        compiler_params=pltpu.CompilerParams(vmem_limit_bytes=8 << 20),
        name="operator",
    )(*[far(x) for x in tables])
    pair_a = lax.ppermute(own, "bx", pairs("bx", 0))
    pair_b = lax.ppermute(own, "bx", pairs("bx", 1))
    corner = jnp.concatenate([from_low, from_high], 0)
    corner_a = lax.ppermute(corner, "bx", pairs("bx", 0))
    corner_b = lax.ppermute(corner, "bx", pairs("bx", 1))
    place = jnp.stack([lax.axis_index("bx") % 2, lax.axis_index("real")]).astype(jnp.int32)
    width = 4 * cols
    span = sy + 1
    energies = cols * sx * sy
    vmem = pl.BlockSpec(memory_space=pltpu.VMEM)
    smem = pl.BlockSpec(memory_space=pltpu.SMEM)
    low_limit = pltpu.CompilerParams(vmem_limit_bytes=16 << 20)
    state_shapes = (
        kept((sx + 3) * width * 3 * span, sz),
        kept((sx + 3) * cols * SLAB, sz),
        kept((sx + 2) * sy, sz),
        kept((sx + 2) * SLAB, sz),
        kept((sx + 2) * SLAB, sz),
        kept((sx + 1) * 3 * SLAB, sz),
        kept(energies, sz),
        kept(energies, sz),
    )
    parts_shape = kept((sx - 1) * cols * 7 * sy, sz)
    *state, parts, prev_parts = pl.pallas_call(
        lambda *refs: early_kernel(sizes, *refs),
        in_specs=[vmem] * 6,
        out_shape=state_shapes + (parts_shape, parts_shape),
        compiler_params=low_limit,
        name="early",
    )(*[near(x) for x in (own, prev_free, from_low, from_high, op_high, op_low)])
    basis, _, stiff, _, _, _, stiff_part, mass_part, applied, a_part, b_part, shared, lumped = pl.pallas_call(
        lambda *refs: current_kernel(sizes, *refs),
        in_specs=[smem] + [vmem] * 15,
        out_shape=state_shapes
        + (
            kept((sx + 1) * width * 3 * span, sz),
            kept(block, sz),
            kept(block, sz),
            kept(energies + 16, sz),
            kept((sx + 1) * SLAB, sz),
        ),
        input_output_aliases={8 + i: i for i in range(8)},
        scratch_shapes=[pltpu.VMEM((16, sz), f32), pltpu.VMEM((16, sz), f32)],
        compiler_params=low_limit,
        name="current",
    )(place, *[near(x) for x in (pair_a, pair_b, corner_a, corner_b, op_high, op_low, parts, *state)])
    count = lax.axis_size("real")
    other = lax.ppermute(shared, "real", [(i, (i + 1) % count) for i in range(count)])
    _, gram = pl.pallas_call(
        lambda *refs: gram_kernel(sizes, *refs),
        in_specs=[vmem] * 7,
        out_shape=(kept((sx + 1) * width * 3 * span, sz), kept(2 * cols, 128)),
        input_output_aliases={6: 0},
        compiler_params=low_limit,
        name="gram",
    )(*[near(x) for x in (basis, stiff, lumped, op_high, op_low, prev_parts, applied)])
    gram = jnp.concatenate([gram[0:16] + other[energies:], gram[16:]], 0)
    gram = sum_over(sum_over(gram, "bx"), "by")
    stiff_gram, mass_gram, search, sensitivity = pl.pallas_call(
        lambda *refs: finish_kernel(sizes, dof, *refs),
        in_specs=[smem] + [vmem] * 6,
        out_shape=(
            struct(3 * cols, 1, 3 * cols),
            struct(3 * cols, 1, 3 * cols),
            struct(1, cols, 3, sx, sy, sz),
            struct(sx, sy, sz // 2),
        ),
        compiler_params=pltpu.CompilerParams(vmem_limit_bytes=12 << 20),
        name="finish",
    )(place, *[near(x) for x in (gram, a_part, b_part, stiff_part, mass_part, other)])
    return jnp.swapaxes(stiff_gram, 0, 1), jnp.swapaxes(mass_gram, 0, 1), search, sensitivity


def solution(mesh):
    in_specs = (
        P("real", None, None, "bx", "by", None),
        P("real", None, None, "bx", "by", None),
        P(),
        P("real", None, "bx", "by", None),
        P("bx", "by", None),
        P("bx", "by", None),
        P("real", "bx", "by", None),
        P("bx", "by"),
    )
    out_specs = (
        P("real", None, None),
        P("real", None, None),
        P("real", None, None, "bx", "by", None),
        P("bx", "by", "real"),
    )
    return jax.shard_map(shards, mesh=mesh, in_specs=in_specs, out_specs=out_specs, check_vma=False)
```
